32 devices in a mesh: fsdp: 4 (over z), context: 2 (over core), tensor: 4 (over y, x).
Axes of the slice: x: 2, y: 2, z: 4, core: 2. Of those that a mesh axis runs over, the one named last changes fastest.
Arguments:
- tokens: bfloat16 [4, 1024, 1536], P('fsdp', 'context'), may hold values from -6 to 6
- segments: int32 [4, 1024], P('fsdp', 'context'), may hold values from 0 to 7, never falling along the last dimension, each value on 1 to 768 neighbouring positions
- cotangent: bfloat16 [4, 1024, 1536], P('fsdp', 'context'), may hold values from -6 to 6
- query_weight: bfloat16 [1536, 1536], P('fsdp', 'tensor'), may hold values from -0.15625 to 0.15625
- key_weight: bfloat16 [1536, 1536], P('fsdp', 'tensor'), may hold values from -0.15625 to 0.15625
- value_weight: bfloat16 [1536, 1536], P('fsdp', 'tensor'), may hold values from -0.15625 to 0.15625
- house_weight: bfloat16 [1536, 1536], P('fsdp', 'tensor'), may hold values from -0.15625 to 0.15625
- beta_weight: bfloat16 [1536, 12], P('fsdp', 'tensor'), may hold values from -0.15625 to 0.15625
- conv_weight: bfloat16 [12, 4, 128], P('tensor', None, 'fsdp'), may hold values from -3 to 3
- output_weight: bfloat16 [1536, 1536], P('tensor', 'fsdp'), may hold values from -0.625 to 0.625
- gate_weight: bfloat16 [1536, 4096], P('fsdp', 'tensor'), may hold values from -0.15625 to 0.15625
- up_weight: bfloat16 [1536, 4096], P('fsdp', 'tensor'), may hold values from -0.15625 to 0.15625
- down_weight: bfloat16 [4096, 1536], P('tensor', 'fsdp'), may hold values from -0.09375 to 0.09375
- first_gain: bfloat16 [1536], P('fsdp'), may hold values from 0.5 to 1.5
- second_gain: bfloat16 [1536], P('fsdp'), may hold values from 0.5 to 1.5
Outputs:
- result: bfloat16 [4, 1024, 1536], P('fsdp', 'context')
- grad_input: float32 [4, 1024, 1536], P('fsdp', 'context')
- grad_query: float32 [1536, 1536], P('fsdp', 'tensor')
- grad_key: float32 [1536, 1536], P('fsdp', 'tensor')
- grad_value: float32 [1536, 1536], P('fsdp', 'tensor')
- grad_house: float32 [1536, 1536], P('fsdp', 'tensor')
- grad_beta: float32 [1536, 12], P('fsdp', 'tensor')
- grad_conv: float32 [12, 4, 128], P('tensor', None, 'fsdp')
- grad_output: float32 [1536, 1536], P('tensor', 'fsdp')
- grad_gate: float32 [1536, 4096], P('fsdp', 'tensor')
- grad_up: float32 [1536, 4096], P('fsdp', 'tensor')
- grad_down: float32 [4096, 1536], P('tensor', 'fsdp')
- grad_first: float32 [1536], P('fsdp')
- grad_second: float32 [1536], P('fsdp')
The draws below stay inside these ranges and needn't reach their ends.
Inputs may be any that keep to these rules, and one draw needn't show every extreme that they name: `segments`: within each sequence the document numbers never fall, every number from 0 to 7 occurs, each document has 1 to 768 tokens, and one document of each sequence has exactly 768.
All inputs are finite; a program needn't handle non-finite values.
Results may differ from the reference program's by a relative error of at most 0.02.
Values may be sent and summed in bfloat16 or wider, within the bound.
A program may use at most 192 MiB of HBM per device.

```python
import math
from functools import partial
import jax
import jax.numpy as jnp
import numpy as np
from jax import lax

D = 1536
HEADS = 12
DH = 128
FF = 4096
KS = 4
LENGTH = 1024
DOCS = 8
HD = 1536
SEQS = 4
MOSTDOC = 768
N_CONTEXT = 2


def levels(stream_key, shape, cuts, least, largest):
    level = 1.0
    for dim, shards_of in cuts:
        draws = jax.random.uniform(jax.random.fold_in(jax.random.fold_in(stream_key, 6), dim), (shards_of,), jnp.float32, least / len(cuts), largest / len(cuts))
        level = level * jnp.repeat(jnp.exp(draws), shape[dim] // shards_of).reshape((-1,) + (1,) * (len(shape) - 1 - dim))
    return level


def split_up(count, total, bound, skew):
    weights = [(1 << 20) // math.isqrt(rank ** skew) + 1 for rank in range(2, count + 1)]
    rest, given = total - bound - (count - 1), [1] * (count - 1)
    while rest > 0:
        candidates = [i for i in range(count - 1) if given[i] < bound]
        mass, remaining = sum([weights[i] for i in candidates]), rest
        for i in candidates:
            more = min(bound - given[i], max(1, remaining * weights[i] // mass), rest)
            given[i] = given[i] + more
            rest = rest - more
    return np.array([bound] + given)


def uneven(key, number_of, total, reach, skew):
    if number_of == 2:
        one = jax.random.randint(key, (), max(1, total - reach), min(reach, total - 1) + 1)
        return jnp.stack([one, total - one])
    lengths = jnp.asarray(split_up(number_of, total, reach, skew), jnp.int32)
    pairs = (number_of - 1) // 2
    source_of, taker = lengths[1:1 + 2 * pairs:2], lengths[2:2 + 2 * pairs:2]
    slack = jnp.minimum(source_of - 1, reach - taker)
    moved = jax.random.randint(jax.random.fold_in(key, 1), (pairs,), 0, 1 << 20) % (slack + 1)
    lengths = lengths.at[1:1 + 2 * pairs:2].set(source_of - moved).at[2:2 + 2 * pairs:2].set(taker + moved)
    return lengths[jax.random.permutation(jax.random.fold_in(key, 2), number_of)]


def noise(key, dims, spread, most, shards=(), kind=jnp.bfloat16):
    array = jax.random.normal(key, dims, jnp.float32) * spread
    if len(shards) > 0:
        array = levels(key, dims, shards, -0.22, 0.18) * array
    return jnp.clip(array, min=-most, max=most).astype(kind)


def setup_inputs(seed: int = 0) -> dict:
    keys = jax.random.split(jax.random.key(seed), 16)
    tokens = noise(keys[0], (SEQS, LENGTH, D), 1.0, 6.0, ((0, 4), (1, 2)))
    segments = jax.vmap(lambda own: jnp.searchsorted(jnp.cumsum(uneven(own, DOCS, LENGTH, MOSTDOC, 2)), jnp.arange(LENGTH), side="right"))(jax.random.split(keys[1], SEQS)).reshape((SEQS, LENGTH)).astype(jnp.int32)
    cotangent = noise(keys[2], (SEQS, LENGTH, D), 1.0, 6.0, ((0, 4), (1, 2)))
    query_weight = noise(keys[3], (D, HD), D ** -0.5, 0.15625, ((0, 4), (1, 4)))
    key_weight = noise(keys[4], (D, HD), D ** -0.5, 0.15625, ((0, 4), (1, 4)))
    value_weight = noise(keys[5], (D, HD), D ** -0.5, 0.15625, ((0, 4), (1, 4)))
    house_weight = noise(keys[6], (D, HD), D ** -0.5, 0.15625, ((0, 4), (1, 4)))
    beta_weight = noise(keys[7], (D, HEADS), D ** -0.5, 0.15625, ((0, 4), (1, 4)))
    conv_weight = noise(keys[8], (HEADS, KS, DH), 0.5, 3.0, ((0, 4), (2, 4)))
    output_weight = noise(keys[9], (HD, D), (D // 16) ** -0.5, 0.625, ((0, 4), (1, 4)))
    gate_weight = noise(keys[10], (D, FF), D ** -0.5, 0.15625, ((0, 4), (1, 4)))
    up_weight = noise(keys[11], (D, FF), D ** -0.5, 0.15625, ((0, 4), (1, 4)))
    down_weight = noise(keys[12], (FF, D), FF ** -0.5, 0.09375, ((0, 4), (1, 4)))
    first_gain = jnp.clip(1.0 + 0.1 * jax.random.normal(keys[13], (D,), jnp.float32), 0.5, 1.5).astype(jnp.bfloat16)
    second_gain = jnp.clip(1.0 + 0.1 * jax.random.normal(keys[14], (D,), jnp.float32), 0.5, 1.5).astype(jnp.bfloat16)
    return {"tokens": tokens, "segments": segments, "cotangent": cotangent, "query_weight": query_weight, "key_weight": key_weight, "value_weight": value_weight, "house_weight": house_weight, "beta_weight": beta_weight, "conv_weight": conv_weight, "output_weight": output_weight, "gate_weight": gate_weight, "up_weight": up_weight, "down_weight": down_weight, "first_gain": first_gain, "second_gain": second_gain}


@jax.custom_vjp
def low(v):
    return lax.optimization_barrier(v.astype(jnp.bfloat16)).astype(jnp.float32)

@jax.custom_vjp
def low_back(v):
    return v

def low_keep(v):
    return (low(v), None)

def low_pass(kept, grad):
    return (grad,)

def back_keep(v):
    return (v, None)

def back_low(kept, grad):
    return (low(grad),)
low.defvjp(low_keep, low_pass)
low_back.defvjp(back_keep, back_low)

def product(former, latter):
    return jnp.dot(former, latter, precision=lax.Precision.HIGHEST)

def rms_scale(values, gain_vec):
    return values * lax.rsqrt(lax.optimization_barrier(jnp.mean(values * values, axis=-1, keepdims=True)) + 1e-06) * gain_vec

def house_conv(values, prefix, kernel, doc_tags, prefix_tags):
    head_total, tap_count, head_width = kernel.shape
    tap_rows = jnp.transpose(kernel, (1, 0, 2)).reshape(tap_count, head_total * head_width)
    joined = jnp.concatenate([prefix, values], axis=values.ndim - 2)
    all_tags = jnp.concatenate([prefix_tags, doc_tags], axis=doc_tags.ndim - 1)
    length = values.shape[-2]
    running = jnp.zeros(values.shape, jnp.float32)
    for offset in range(tap_count):
        offset_at = tap_count - 1 - offset
        shifted = lax.slice_in_dim(joined, offset_at, offset_at + length, axis=joined.ndim - 2)
        shifted_tags = lax.slice_in_dim(all_tags, offset_at, offset_at + length, axis=all_tags.ndim - 1)
        same_doc = (shifted_tags == doc_tags)[..., None]
        running = running + jnp.where(same_doc, shifted, 0.0) * tap_rows[offset]
    activation = jax.nn.silu(running)
    per_head = activation.reshape(activation.shape[:-1] + (head_total, head_width))
    normed = per_head * lax.rsqrt(lax.optimization_barrier(jnp.sum(per_head * per_head, axis=-1, keepdims=True)) + 1e-06)
    return normed.reshape(activation.shape)

def triangle(house_rows, beta_rows, doc_tags):
    length = house_rows.shape[0]
    places = jnp.arange(length)
    earlier = (places[:, None] > places[None, :]) & (doc_tags[:, None] == doc_tags[None, :])
    coupling = jnp.where(earlier, product(house_rows, house_rows.T) * beta_rows[:, None], 0.0)
    return (jnp.eye(length, dtype=jnp.float32) + coupling, earlier)

def trans_keys(key_rows, house_rows, beta_rows, doc_tags):
    system, earlier = triangle(house_rows, beta_rows, doc_tags)
    right_side = jnp.where(earlier, product(house_rows, key_rows.T) * beta_rows[:, None], 0.0)
    solved = jax.scipy.linalg.solve_triangular(system, right_side, lower=True)
    return key_rows - product(solved.T, house_rows)

def attend(queries, key_rows, house_rows, beta_rows, doc_tags, far_keys, far_tags):
    system, earlier = triangle(house_rows, beta_rows, doc_tags)
    length = queries.shape[0]
    places = jnp.arange(length)
    far_same = doc_tags[:, None] == far_tags[None, :]
    local_side = jnp.where(earlier, product(house_rows, key_rows.T) * beta_rows[:, None], 0.0)
    far_side = jnp.where(far_same, product(house_rows, far_keys.T) * beta_rows[:, None], 0.0)
    solved = jax.scipy.linalg.solve_triangular(system, jnp.concatenate([local_side, far_side], axis=1), lower=True)
    causal = places[:, None] >= places[None, :]
    reached = jnp.where(causal, product(queries, house_rows.T), 0.0)
    raw_scores = product(queries, jnp.concatenate([key_rows, far_keys], axis=0).T) - product(reached, solved)
    allowed = jnp.concatenate([causal & (doc_tags[:, None] == doc_tags[None, :]), far_same], axis=1)
    scores = jnp.where(allowed, raw_scores / math.sqrt(queries.shape[1]), -1e+30)
    row_max = lax.optimization_barrier(jnp.max(scores, axis=1, keepdims=True))
    powered = jnp.exp(scores - row_max)
    return powered / lax.optimization_barrier(jnp.sum(powered, axis=1, keepdims=True))

def head_split(values, head_total):
    length, total_width = values.shape
    return jnp.transpose(values.reshape(length, head_total, total_width // head_total), (1, 0, 2))

def head_pass(block_tags, far_tags, item_in):
    queries, key_rows, value_rows, house_rows, beta_rows, far_keys, far_values = item_in
    attn_probs = low(attend(queries, key_rows, house_rows, beta_rows, block_tags, far_keys, far_tags))
    mixed = product(attn_probs, jnp.concatenate([value_rows, far_values], axis=0))
    sent_keys = trans_keys(key_rows, house_rows, beta_rows, block_tags)
    return (mixed, sent_keys)

def sequence_pass(stream, doc_tags, weights):
    query_weight, key_weight, value_weight, house_weight, beta_weight, conv_weight, output_weight, gate_weight, up_weight, down_weight, first_gain, second_gain = weights
    normed = low(rms_scale(stream, first_gain))
    queries = low(low_back(product(normed, query_weight)))
    key_all = low(low_back(product(normed, key_weight)))
    value_all = low(low_back(product(normed, value_weight)))
    house_in = low(low_back(product(normed, house_weight)))
    beta_all = 2.0 * jax.nn.sigmoid(low_back(product(normed, beta_weight)))
    length = LENGTH // N_CONTEXT
    tap_count = conv_weight.shape[1]
    inner_width = queries.shape[1]
    prefix = jnp.zeros((tap_count - 1, inner_width), jnp.float32)
    prefix_tags = jnp.zeros((tap_count - 1,), jnp.float32)
    far_keys = jnp.zeros((HEADS, length, DH), jnp.float32)
    far_values = jnp.zeros((HEADS, length, DH), jnp.float32)
    far_tags = jnp.zeros((length,), jnp.float32)
    pieces = []
    for block_at in range(N_CONTEXT):
        window = slice(block_at * length, (block_at + 1) * length)
        block_tags = doc_tags[window]
        block_in = house_in[window]
        house_rows = low(house_conv(block_in, prefix, conv_weight, block_tags, prefix_tags))
        value_heads = head_split(value_all[window], HEADS)
        mixed, sent_keys = lax.map(jax.checkpoint(partial(head_pass, block_tags, far_tags)), (head_split(queries[window], HEADS), head_split(key_all[window], HEADS), value_heads, head_split(house_rows, HEADS), beta_all[window].T, far_keys, far_values))
        pieces.append(jnp.transpose(mixed, (1, 0, 2)).reshape(length, inner_width))
        far_keys = low_back(low(sent_keys))
        far_values = low_back(value_heads)
        far_tags = block_tags
        prefix = low_back(block_in[length - tap_count + 1:])
        prefix_tags = block_tags[length - tap_count + 1:]
    mixed_all = low(low_back(jnp.concatenate(pieces, axis=0)))
    middle = stream + low_back(product(mixed_all, output_weight))
    normed_two = low(rms_scale(middle, second_gain))
    gate_value = low_back(product(normed_two, gate_weight))
    up_value = low_back(product(normed_two, up_weight))
    hidden = low(jax.nn.silu(gate_value) * up_value)
    return middle + low_back(product(hidden, down_weight))

def reference(tokens, segments, cotangent, query_weight, key_weight, value_weight, house_weight, beta_weight, conv_weight, output_weight, gate_weight, up_weight, down_weight, first_gain, second_gain):
    weights = (query_weight.astype(jnp.float32), key_weight.astype(jnp.float32), value_weight.astype(jnp.float32), house_weight.astype(jnp.float32), beta_weight.astype(jnp.float32), conv_weight.astype(jnp.float32), output_weight.astype(jnp.float32), gate_weight.astype(jnp.float32), up_weight.astype(jnp.float32), down_weight.astype(jnp.float32), first_gain.astype(jnp.float32), second_gain.astype(jnp.float32))
    doc_tags = (segments + 1).astype(jnp.float32)

    def forward(stream, params):

        def one_sequence(item_in):
            return sequence_pass(item_in[0], item_in[1], params)
        return lax.map(jax.checkpoint(one_sequence), (stream, doc_tags))
    result, pullback = jax.vjp(forward, tokens.astype(jnp.float32), weights)
    grad_input, grads = pullback(cotangent.astype(jnp.float32))
    return (result.astype(jnp.bfloat16), grad_input, grads[0], grads[1], grads[2], grads[3], grads[4], grads[5], grads[6], grads[7], grads[8], grads[9], grads[10], grads[11])
```

```python
import functools
import math

import jax
import jax.numpy as jnp
from jax import lax
from jax.experimental import pallas as pl
from jax.experimental.pallas import tpu as pltpu
from jax.sharding import PartitionSpec as P

BF = jnp.bfloat16
F32 = jnp.float32
HALO = 16


def dot_nn(a, b):
    return jnp.dot(a, b, preferred_element_type=F32)


def dot_nt(a, b):
    return lax.dot_general(a, b, (((1,), (1,)), ((), ())), preferred_element_type=F32)


def dot_tn(a, b):
    return lax.dot_general(a, b, (((0,), (0,)), ((), ())), preferred_element_type=F32)


def iotas(rows, cols):
    return (
        lax.broadcasted_iota(jnp.int32, (rows, cols), 0),
        lax.broadcasted_iota(jnp.int32, (rows, cols), 1),
    )


def unit_lower_inverse(blocks, size):
    row, col = iotas(size, size)
    diff = row ^ col
    eye = jnp.where(row == col, 1.0, 0.0).astype(F32)
    low = row > col
    inv = [eye - jnp.where(low & (diff < 2), a, 0.0) for a in blocks]
    span = 2
    while span < size:
        pick = low & (diff >= span) & (diff < 2 * span)
        off = [jnp.where(pick, a, 0.0).astype(BF) for a in blocks]
        held = [t.astype(BF) for t in inv]
        step = [dot_nn(h, o).astype(BF) for h, o in zip(held, off)]
        inv = [t - dot_nn(s, h) for t, s, h in zip(inv, step, held)]
        span *= 2
    return inv


def conv_taps(hin, prefix, taps, marks):
    ext = jnp.concatenate([prefix, hin], axis=0)
    shifts = [hin]
    total = hin * taps[0:1, :]
    for lag in range(1, taps.shape[0]):
        moved = pltpu.roll(ext, lag, 0)[HALO:, :]
        moved = jnp.where(marks[:, lag : lag + 1] > 0.0, moved, 0.0)
        shifts.append(moved)
        total = total + moved * taps[lag : lag + 1, :]
    return total, shifts


def prep_kernel(k_ref, h_ref, pre_ref, tap_ref, mark_ref, b_ref, w_ref, t_ref, c_ref, sent_ref):
    length = k_ref.shape[0]
    half = length // 2
    quarter = length // 4
    heads = t_ref.shape[0]
    row, col = iotas(length, length)
    strict = row > col
    total, unused = conv_taps(
        h_ref[...].astype(F32), pre_ref[...].astype(F32), tap_ref[...], mark_ref[...]
    )
    act = total * jax.nn.sigmoid(total)
    houses, blocks, coupled = [], [], []
    for h in range(heads):
        cols = slice(h * 128, (h + 1) * 128)
        a = act[:, cols]
        w = (a * lax.rsqrt(jnp.sum(a * a, axis=1, keepdims=True) + 1e-06)).astype(BF)
        w_ref[:, cols] = w
        houses.append(w)
        full = jnp.where(strict, dot_nt(w, w) * b_ref[:, h * 128 : h * 128 + 1], 0.0)
        coupled.append(full.astype(BF))
        for q in range(4):
            blocks.append(full[q * quarter : (q + 1) * quarter, q * quarter : (q + 1) * quarter])
    inv = unit_lower_inverse(blocks, quarter)
    for h in range(heads):
        cols = slice(h * 128, (h + 1) * 128)
        diag = [t.astype(BF) for t in inv[4 * h : 4 * h + 4]]
        halves = []
        for p in range(2):
            at = p * half
            off = coupled[h][at + quarter : at + half, at : at + quarter]
            corner = -dot_nn(dot_nn(diag[2 * p + 1], off).astype(BF), diag[2 * p])
            zero = jnp.zeros((quarter, quarter), BF)
            halves.append(
                jnp.concatenate(
                    [
                        jnp.concatenate([diag[2 * p], zero], axis=1),
                        jnp.concatenate([corner.astype(BF), diag[2 * p + 1]], axis=1),
                    ],
                    axis=0,
                )
            )
        off = coupled[h][half:, :half]
        corner = -dot_nn(dot_nn(halves[1], off).astype(BF), halves[0])
        t_full = jnp.concatenate(
            [
                jnp.concatenate([halves[0], jnp.zeros((half, half), BF)], axis=1),
                jnp.concatenate([corner.astype(BF), halves[1]], axis=1),
            ],
            axis=0,
        )
        t_ref[h] = t_full
        w = houses[h]
        k = k_ref[:, cols]
        c = jnp.where(strict, dot_nt(w, k) * b_ref[:, h * 128 : h * 128 + 1], 0.0).astype(BF)
        c_ref[h] = c
        z = dot_tn(t_full, w).astype(BF)
        sent_ref[:, cols] = (k.astype(F32) - dot_tn(c, z)).astype(BF)


def attend_kernel(
    q_ref, k_ref, v_ref, w_ref, b_ref, t_ref, c_ref, fk_ref, fv_ref, tc_ref, tr_ref,
    o_ref, p_ref, x_ref, qt_ref,
):
    length = q_ref.shape[0]
    row, col = iotas(length, length)
    causal = row >= col
    q, k, w = q_ref[...], k_ref[...], w_ref[...]
    wb = (w.astype(F32) * b_ref[...]).astype(BF)
    reach = jnp.where(causal, dot_nt(q, w), 0.0).astype(BF)
    x = dot_nn(reach, t_ref[0]).astype(BF)
    x_ref[0] = x
    qt = (q.astype(F32) - dot_nn(x, wb)).astype(BF)
    qt_ref[...] = qt
    scale = 1.0 / math.sqrt(q.shape[1])
    tags = tc_ref[...]
    near = jnp.where(
        causal & (tags == tr_ref[0:1, :]), (dot_nt(q, k) - dot_nn(x, c_ref[0])) * scale, -1e30
    )
    far = jnp.where(tags == tr_ref[1:2, :], dot_nt(qt, fk_ref[...]) * scale, -1e30)
    top = jnp.maximum(
        jnp.max(near, axis=1, keepdims=True), jnp.max(far, axis=1, keepdims=True)
    )
    near = jnp.exp(near - top)
    far = jnp.exp(far - top)
    inv = 1.0 / (jnp.sum(near, axis=1, keepdims=True) + jnp.sum(far, axis=1, keepdims=True))
    near = (near * inv).astype(BF)
    far = (far * inv).astype(BF)
    p_ref[0, :, :length] = near
    p_ref[0, :, length:] = far
    o_ref[...] = (dot_nn(near, v_ref[...]) + dot_nn(far, fv_ref[...])).astype(BF)


def attend_back_kernel(
    g_ref, q_ref, k_ref, v_ref, w_ref, b_ref, t_ref, c_ref, fk_ref, fv_ref, p_ref, x_ref, qt_ref,
    dq_ref, dk_ref, dv_ref, dw_ref, dwb_ref, dfk_ref, dfv_ref,
):
    length = q_ref.shape[0]
    row, col = iotas(length, length)
    q, k, w, g = q_ref[...], k_ref[...], w_ref[...], g_ref[...]
    wb = (w.astype(F32) * b_ref[...]).astype(BF)
    x, t, c = x_ref[0], t_ref[0], c_ref[0]
    near, far = p_ref[0, :, :length], p_ref[0, :, length:]
    dv_ref[...] = dot_tn(near, g)
    dfv_ref[...] = dot_tn(far, g).astype(BF)
    d_near = dot_nt(g, v_ref[...])
    d_far = dot_nt(g, fv_ref[...])
    near, far = near.astype(F32), far.astype(F32)
    mean = jnp.sum(near * d_near, axis=1, keepdims=True) + jnp.sum(
        far * d_far, axis=1, keepdims=True
    )
    scale = 1.0 / math.sqrt(q.shape[1])
    s_near = (near * (d_near - mean) * scale).astype(BF)
    s_far = (far * (d_far - mean) * scale).astype(BF)
    dfk_ref[...] = dot_tn(s_far, qt_ref[...]).astype(BF)
    dqt = dot_nn(s_far, fk_ref[...])
    dqt_low = dqt.astype(BF)
    neg_dx = (dot_nt(s_near, c) + dot_nt(dqt_low, wb)).astype(BF)
    e = jnp.where(row >= col, -dot_nt(neg_dx, t), 0.0).astype(BF)
    dc = jnp.where(row > col, -dot_tn(x, s_near), 0.0).astype(BF)
    da = jnp.where(row > col, -dot_tn(x, e), 0.0).astype(BF)
    dq = dot_nn(
        jnp.concatenate([s_near, s_far, e], axis=1),
        jnp.concatenate([k, fk_ref[...], w], axis=0),
    )
    dq_ref[...] = dq.astype(BF)
    dk_ref[...] = dot_tn(s_near, q) + dot_tn(dc, wb)
    dwb_ref[...] = dot_nn(dc, k) - dot_tn(x, dqt_low) + dot_nn(da, w)
    dw_ref[...] = dot_tn(e, q) + dot_tn(da, wb)


def keys_back_kernel(
    d_ref, bv_ref, q_ref, k_ref, w_ref, b_ref, t_ref, c_ref, h_ref, pre_ref, tap_ref, mark_ref,
    dki_ref, dvi_ref, dwi_ref, dwbi_ref,
    out_ref, tail_ref, dpre_ref, dtap_ref,
):
    length, inner = k_ref.shape
    heads = inner // 128
    row, col = iotas(length, length)
    strict = row > col
    marks = mark_ref[...]
    lanes = lax.broadcasted_iota(jnp.int32, (length, 128), 1)
    side = jnp.zeros((length, 128), F32)
    out_ref[:, :inner] = q_ref[...]
    out_ref[:, 2 * inner : 3 * inner] = (dvi_ref[...] + bv_ref[...].astype(F32)).astype(BF)
    for h in range(heads):
        cols = slice(h * 128, (h + 1) * 128)
        k, w, d, b = k_ref[:, cols], w_ref[:, cols], d_ref[:, cols], b_ref[:, cols]
        wb = (w.astype(F32) * b).astype(BF)
        t, c = t_ref[h], c_ref[h]
        z = dot_tn(t, w).astype(BF)
        dc = jnp.where(strict, -dot_nt(z, d), 0.0).astype(BF)
        f = -dot_nn(t, dot_nn(c, d).astype(BF))
        da = jnp.where(strict, -dot_nt(z, f.astype(BF)), 0.0).astype(BF)
        dk = (dki_ref[:, cols] + d.astype(F32) + dot_tn(dc, wb)).astype(BF)
        out_ref[:, inner + h * 128 : inner + (h + 1) * 128] = dk
        dwb = dwbi_ref[:, cols] + dot_nn(dc, k) + dot_nn(da, w)
        dw = dwi_ref[:, cols] + f + dot_tn(da, wb) + b * dwb
        db = jnp.sum(dwb * w.astype(F32), axis=1, keepdims=True)
        side = jnp.where(lanes == h, db * (b * (1.0 - 0.5 * b)), side)
        taps = tap_ref[:, cols]
        total, shifts = conv_taps(
            h_ref[:, cols].astype(F32), pre_ref[:, cols].astype(F32), taps, marks
        )
        sig = jax.nn.sigmoid(total)
        act = total * sig
        r = lax.rsqrt(jnp.sum(act * act, axis=1, keepdims=True) + 1e-06)
        d_act = r * dw - act * (r * r * r * jnp.sum(act * dw, axis=1, keepdims=True))
        d_total = d_act * sig * (1.0 + total * (1.0 - sig))
        rows = [jnp.sum(d_total * s, axis=0, keepdims=True) for s in shifts]
        dtap_ref[:, cols] = jnp.concatenate(
            rows + [jnp.zeros((8 - len(rows), 128), F32)], axis=0
        )
        pad = jnp.zeros((HALO, 128), F32)
        out = jnp.concatenate([pad, d_total * taps[0:1, :]], axis=0)
        for lag in range(1, taps.shape[0]):
            part = jnp.where(marks[:, lag : lag + 1] > 0.0, d_total, 0.0) * taps[lag : lag + 1, :]
            out = out + pltpu.roll(jnp.concatenate([pad, part], axis=0), length + HALO - lag, 0)
        dpre_ref[:, cols] = out[:HALO, :].astype(BF)
        tail_ref[:, cols] = out[length:, :]
        out_ref[:, 3 * inner + h * 128 : 3 * inner + (h + 1) * 128] = out[HALO:, :].astype(BF)
    out_ref[:, 4 * inner :] = side.astype(BF)


def sds(shape, dtype):
    return jax.ShapeDtypeStruct(shape, dtype)


def cost(micros):
    return pl.CostEstimate(flops=micros * 10**9, bytes_accessed=micros * 10**6, transcendentals=0)


def params():
    return pltpu.CompilerParams(vmem_limit_bytes=56 * 1024 * 1024)


def call_prep(k, hin, prefix, taps, marks, beta):
    length, width = k.shape
    heads = width // 128
    whole = pl.BlockSpec(memory_space=pltpu.VMEM)
    return pl.pallas_call(
        prep_kernel,
        out_shape=(
            sds((length, width), BF),
            sds((heads, length, length), BF),
            sds((heads, length, length), BF),
            sds((length, width), BF),
        ),
        in_specs=[whole] * 6,
        out_specs=[whole] * 4,
        compiler_params=params(),
        cost_estimate=cost(9),
        name="prep",
    )(k, hin, prefix, taps, marks, beta)


def head_specs(length):
    slab = pl.BlockSpec((length, 128), lambda h: (0, h))
    square = pl.BlockSpec((1, length, length), lambda h: (h, 0, 0))
    double = pl.BlockSpec((1, length, 2 * length), lambda h: (h, 0, 0))
    return slab, square, double


def fixed(shape):
    return pl.BlockSpec(shape, lambda h: (0,) * len(shape))


def call_attend(q, k, v, w, beta, t, c, fk, fv, tag_col, tag_rows):
    length, width = q.shape
    heads = width // 128
    slab, square, double = head_specs(length)
    return pl.pallas_call(
        attend_kernel,
        grid=(heads,),
        out_shape=(
            sds((length, width), BF),
            sds((heads, length, 2 * length), BF),
            sds((heads, length, length), BF),
            sds((length, width), BF),
        ),
        in_specs=[slab] * 5
        + [square, square, slab, slab, fixed(tag_col.shape), fixed(tag_rows.shape)],
        out_specs=[slab, double, square, slab],
        compiler_params=params(),
        cost_estimate=cost(11),
        name="attend",
    )(q, k, v, w, beta, t, c, fk, fv, tag_col, tag_rows)


def call_attend_back(g, q, k, v, w, beta, t, c, fk, fv, p, x, qt):
    length, width = q.shape
    heads = width // 128
    slab, square, double = head_specs(length)
    flat = (length, width)
    return pl.pallas_call(
        attend_back_kernel,
        grid=(heads,),
        out_shape=(
            sds(flat, BF), sds(flat, F32), sds(flat, F32), sds(flat, F32), sds(flat, F32),
            sds(flat, BF), sds(flat, BF),
        ),
        in_specs=[slab] * 6 + [square, square, slab, slab, double, square, slab],
        out_specs=[slab] * 7,
        compiler_params=params(),
        cost_estimate=cost(16),
        name="attend_back",
    )(g, q, k, v, w, beta, t, c, fk, fv, p, x, qt)


def call_keys_back(d, back_v, dq, k, w, beta, t, c, hin, prefix, taps, marks, dk, dv, dw, dwb):
    length, width = k.shape
    whole = pl.BlockSpec(memory_space=pltpu.VMEM)
    return pl.pallas_call(
        keys_back_kernel,
        out_shape=(
            sds((length, 4 * width + 128), BF), sds((HALO, width), F32), sds((HALO, width), BF),
            sds((8, width), F32),
        ),
        in_specs=[whole] * 16,
        out_specs=[whole] * 4,
        compiler_params=params(),
        cost_estimate=cost(10),
        name="keys_back",
    )(d, back_v, dq, k, w, beta, t, c, hin, prefix, taps, marks, dk, dv, dw, dwb)


def exchange(mesh_size, name, ident, lhs, rhs, transposed, extras, finish, rows_out, wide_type):
    length = lhs.shape[0]
    model = rhs.shape[0] if transposed else rhs.shape[1]
    n = mesh_size
    chunk = length // n
    many = len(extras)

    def body(*refs):
        lhs_ref, rhs_ref = refs[:2]
        extra_refs = refs[2 : 2 + many]
        out_ref, *row_refs = refs[2 + many : 3 + many + len(rows_out)]
        send, recv, held, send_a, recv_a, send_b, recv_b = refs[3 + many + len(rows_out) :]
        me = lax.axis_index("tensor")
        barrier = pltpu.get_barrier_semaphore()
        peers = [lax.rem(me + i, n) for i in range(1, n)]
        for peer in peers:
            pl.semaphore_signal(
                barrier, inc=1, device_id={"tensor": peer}, device_id_type=pl.DeviceIdType.MESH
            )
        pl.semaphore_wait(barrier, n - 1)

        def rows_of(index):
            return pl.ds(pl.multiple_of(index * chunk, chunk), chunk)

        def partial(index):
            left = lhs_ref[rows_of(index), :]
            return dot_nt(left, rhs_ref[...]) if transposed else dot_nn(left, rhs_ref[...])

        first = []
        for i, peer in enumerate(peers):
            send[i] = partial(peer).astype(BF)
            copy = pltpu.make_async_remote_copy(
                src_ref=send.at[i], dst_ref=recv.at[i],
                send_sem=send_a.at[i], recv_sem=recv_a.at[i],
                device_id={"tensor": peer}, device_id_type=pl.DeviceIdType.MESH,
            )
            copy.start()
            first.append(copy)
        total = partial(me)
        for i, copy in enumerate(first):
            copy.wait()
            total = total + recv[i].astype(F32)
        mine = rows_of(me)
        done, *row_values = finish(total, mine, *extra_refs)
        held[mine, :] = done.astype(BF)
        second = []
        for i, peer in enumerate(peers):
            copy = pltpu.make_async_remote_copy(
                src_ref=held.at[mine, :], dst_ref=held.at[mine, :],
                send_sem=send_b.at[i], recv_sem=recv_b.at[i],
                device_id={"tensor": peer}, device_id_type=pl.DeviceIdType.MESH,
            )
            copy.start()
            second.append(copy)
        for ref, value in zip(row_refs, row_values):
            ref[...] = value
        for copy in second:
            copy.wait()
        out_ref[...] = held[...].astype(wide_type)

    whole = pl.BlockSpec(memory_space=pltpu.VMEM)
    return pl.pallas_call(
        body,
        out_shape=(sds((length, model), wide_type),)
        + tuple(sds((chunk if r is None else r, model), F32) for r in rows_out),
        in_specs=[whole] * (2 + many),
        out_specs=[whole] * (1 + len(rows_out)),
        scratch_shapes=[
            pltpu.VMEM((n - 1, chunk, model), BF),
            pltpu.VMEM((n - 1, chunk, model), BF),
            pltpu.VMEM((length, model), BF),
            pltpu.SemaphoreType.DMA((n - 1,)),
            pltpu.SemaphoreType.DMA((n - 1,)),
            pltpu.SemaphoreType.DMA((n - 1,)),
            pltpu.SemaphoreType.DMA((n - 1,)),
        ],
        compiler_params=pltpu.CompilerParams(
            vmem_limit_bytes=56 * 1024 * 1024, collective_id=ident, has_side_effects=True
        ),
        cost_estimate=cost(40),
        name=name,
    )(lhs, rhs, *extras)


def inverse_rms(x):
    return lax.rsqrt(jnp.mean(x * x, axis=1, keepdims=True) + 1e-06)


def finish_middle(total, mine, tokens_ref, gain_ref):
    middle = tokens_ref[mine, :].astype(F32) + total
    return middle * inverse_rms(middle) * gain_ref[0:1, :], middle


def finish_result(total, mine, middle_ref):
    return (middle_ref[...] + total,)


def norm_back(grad, x, gain):
    r = inverse_rms(x)
    g = grad * gain
    out = r * g - x * (r * r * r * jnp.mean(g * x, axis=1, keepdims=True))
    gain_grad = jnp.sum(grad * x * r, axis=0, keepdims=True)
    return out, jnp.broadcast_to(gain_grad, (8, gain_grad.shape[1]))


def finish_second(total, mine, middle_ref, cot_ref, gain_ref):
    out, gain_grad = norm_back(total, middle_ref[...], gain_ref[0:1, :])
    grad = cot_ref[mine, :].astype(F32) + out
    return grad, grad, gain_grad


def finish_first(total, mine, tokens_ref, grad_ref, gain_ref):
    out, gain_grad = norm_back(total, tokens_ref[mine, :].astype(F32), gain_ref[0:1, :])
    return grad_ref[...] + out, gain_grad


def shift_to(value, axis, steps):
    count = lax.axis_size(axis)
    leading, last = (max(0, -steps), min(count, count - steps))
    return lax.ppermute(value, axis, [(at, at + steps) for at in range(leading, last)])


def own_half(value):
    rows = value.shape[0] // lax.axis_size("context")
    return lax.dynamic_slice_in_dim(value, lax.axis_index("context") * rows, rows, axis=0)


def gather_rows(value):
    return lax.all_gather(own_half(value), ("fsdp", "context"), axis=0, tiled=True)


def gather_cols(value):
    rows, cols = value.shape
    deep, cores = lax.axis_size("fsdp"), lax.axis_size("context")
    parts = lax.all_gather(own_half(value), ("fsdp", "context"), axis=0, tiled=True)
    parts = parts.reshape(deep, rows, cols)
    return jnp.transpose(parts, (1, 0, 2)).reshape(rows, deep * cols)


def scatter_rows(value):
    part = lax.psum_scatter(value, ("fsdp", "context"), scatter_dimension=0, tiled=True)
    return lax.all_gather(part, "context", axis=0, tiled=True)


def scatter_cols(value):
    rows, cols = value.shape
    deep = lax.axis_size("fsdp")
    parts = jnp.transpose(value.reshape(rows, deep, cols // deep), (1, 0, 2))
    return scatter_rows(parts.reshape(deep * rows, cols // deep))


def on_device(
    tokens,
    segments,
    cotangent,
    query_weight,
    key_weight,
    value_weight,
    house_weight,
    beta_weight,
    conv_weight,
    output_weight,
    gate_weight,
    up_weight,
    down_weight,
    first_gain,
    second_gain,
):
    seq_count, length, model = tokens.shape
    rows = first_gain.shape[0]
    deep = lax.axis_size("fsdp")
    inner = query_weight.shape[1]
    heads, tap_count, chans = conv_weight.shape
    assert seq_count == 1 and heads * tap_count * chans == rows
    side = jnp.concatenate(
        [
            beta_weight,
            first_gain[:, None],
            second_gain[:, None],
            conv_weight.reshape(rows, 1),
            jnp.zeros((rows, 128 - heads - 3), BF),
        ],
        axis=1,
    )
    pack = gather_rows(
        jnp.concatenate([query_weight, key_weight, value_weight, house_weight, side], axis=1)
    )
    out_down = gather_cols(jnp.concatenate([output_weight, down_weight], axis=0))
    gate_up = gather_rows(jnp.concatenate([gate_weight, up_weight], axis=1))
    output_full, down_full = out_down[:inner], out_down[inner:]
    side_full = pack[:, 4 * inner :]
    gain_one = side_full[:, heads].astype(F32)
    gain_two = side_full[:, heads + 1].astype(F32)
    taps = jnp.transpose(
        side_full[:, heads + 2].reshape(deep, heads, tap_count, chans), (2, 1, 0, 3)
    ).reshape(tap_count, inner).astype(F32)

    tags = (segments[0] + 1).astype(F32)
    far_tags = shift_to(tags, "context", 1)
    near_tags = jnp.concatenate([far_tags[length - tap_count + 1 :], tags])
    marks = jnp.stack(
        [
            near_tags[tap_count - 1 - lag : tap_count - 1 - lag + length] == tags
            for lag in range(tap_count)
        ],
        axis=1,
    ).astype(F32)

    stream = tokens[0].astype(F32)
    scale_one = lax.rsqrt(jnp.mean(stream * stream, axis=1, keepdims=True) + 1e-06)
    normed = (stream * scale_one * gain_one).astype(BF)
    proj = dot_nn(normed, pack[:, : 4 * inner]).astype(BF)
    beta_raw = dot_nn(normed, side_full)[:, :heads]
    beta = jnp.repeat(2.0 * jax.nn.sigmoid(beta_raw), 128, axis=1)
    q, k, v, hin = (proj[:, i * inner : (i + 1) * inner] for i in range(4))
    prefix = shift_to(hin[length - HALO :], "context", 1)
    w, t, c, sent = call_prep(k, hin, prefix, taps, marks, beta)
    far_k = shift_to(sent, "context", 1)
    far_v = shift_to(v, "context", 1)
    mixed, probs, x, qt = call_attend(
        q, k, v, w, beta, t, c, far_k, far_v, tags[:, None], jnp.stack([tags, far_tags])
    )
    n = lax.axis_size("tensor")
    rows_one = jnp.broadcast_to(gain_one[None, :], (8, model))
    rows_two = jnp.broadcast_to(gain_two[None, :], (8, model))
    normed_two, middle = exchange(
        n, "sum_mixed", 1, mixed, output_full, False, (tokens[0], rows_two), finish_middle,
        (None,), BF,
    )

    both = dot_nn(normed_two, gate_up)
    hidden_width = both.shape[1] // 2
    gate, up = both[:, :hidden_width], both[:, hidden_width:]
    sig = jax.nn.sigmoid(gate)
    act = gate * sig
    hidden = (act * up).astype(BF)
    grad_rows = cotangent[0]
    grad_hidden = dot_nt(grad_rows, down_full)
    grad_both = jnp.concatenate(
        [grad_hidden * up * (sig + act * (1.0 - sig)), grad_hidden * act], axis=1
    ).astype(BF)
    grad_down = scatter_cols(dot_tn(hidden, grad_rows).astype(BF))
    grad_gate_up = scatter_rows(dot_tn(normed_two, grad_both).astype(BF))
    grad_attn, grad_middle, grad_second = exchange(
        n, "sum_second", 2, grad_both, gate_up, True, (middle, grad_rows, rows_two),
        finish_second, (None, 8), BF,
    )
    grad_output = scatter_cols(dot_tn(mixed, grad_attn).astype(BF))
    grad_mixed = dot_nt(grad_attn, output_full).astype(BF)

    dq, dk, dv, dw, dwb, dfk, dfv = call_attend_back(
        grad_mixed, q, k, v, w, beta, t, c, far_k, far_v, probs, x, qt
    )
    back_k = shift_to(dfk, "context", -1)
    back_v = shift_to(dfv, "context", -1)
    dproj, tail, dpre, dtap = call_keys_back(
        back_k, back_v, dq, k, w, beta, t, c, hin, prefix, taps, marks, dk, dv, dw, dwb
    )
    back_pre = shift_to(dpre, "context", -1).astype(F32)
    dproj = lax.dynamic_update_slice(
        dproj, (tail + back_pre).astype(BF), (length - HALO, 3 * inner)
    )
    grad_input, grad_first = exchange(
        n, "sum_first", 3, dproj, pack, True, (tokens[0], grad_middle, rows_one),
        finish_first, (8,), F32,
    )
    (result,) = exchange(
        n, "sum_hidden", 4, hidden, down_full, False, (middle,), finish_result, (), BF
    )
    grad_pack = dot_tn(normed, dproj).astype(BF)
    dconv = jnp.transpose(
        dtap[:tap_count].reshape(tap_count, heads, deep, chans), (2, 1, 0, 3)
    ).reshape(model, 1)
    side_cols = lax.broadcasted_iota(jnp.int32, (model, 128), 1)
    side_back = jnp.where(
        side_cols == heads + 2, dconv.astype(BF), grad_pack[:, 4 * inner :]
    )
    shares = scatter_rows(
        jnp.concatenate([grad_pack[:, : 4 * inner], side_back], axis=1)
    ).astype(F32)
    gains = lax.psum(
        jnp.stack([grad_first[0], grad_second[0]]), ("fsdp", "context", "tensor")
    )
    gains = lax.dynamic_slice_in_dim(gains, lax.axis_index("fsdp") * rows, rows, axis=1)
    grad_gate_up = grad_gate_up.astype(F32)
    return (
        result.reshape(tokens.shape),
        grad_input.reshape(tokens.shape),
        shares[:, :inner],
        shares[:, inner : 2 * inner],
        shares[:, 2 * inner : 3 * inner],
        shares[:, 3 * inner : 4 * inner],
        shares[:, 4 * inner : 4 * inner + heads],
        shares[:, 4 * inner + heads + 2].reshape(conv_weight.shape),
        grad_output.astype(F32),
        grad_gate_up[:, :hidden_width],
        grad_gate_up[:, hidden_width:],
        grad_down.astype(F32),
        gains[0],
        gains[1],
    )


def solution(mesh):
    in_specs = (
        P("fsdp", "context", None),
        P("fsdp", "context"),
        P("fsdp", "context", None),
        P("fsdp", "tensor"),
        P("fsdp", "tensor"),
        P("fsdp", "tensor"),
        P("fsdp", "tensor"),
        P("fsdp", "tensor"),
        P("tensor", None, "fsdp"),
        P("tensor", "fsdp"),
        P("fsdp", "tensor"),
        P("fsdp", "tensor"),
        P("tensor", "fsdp"),
        P("fsdp"),
        P("fsdp"),
    )
    out_specs = (
        P("fsdp", "context", None),
        P("fsdp", "context", None),
        P("fsdp", "tensor"),
        P("fsdp", "tensor"),
        P("fsdp", "tensor"),
        P("fsdp", "tensor"),
        P("fsdp", "tensor"),
        P("tensor", None, "fsdp"),
        P("tensor", "fsdp"),
        P("fsdp", "tensor"),
        P("fsdp", "tensor"),
        P("tensor", "fsdp"),
        P("fsdp"),
        P("fsdp"),
    )
    return jax.shard_map(
        on_device, mesh=mesh, in_specs=in_specs, out_specs=out_specs, check_vma=False
    )
```

```python
import functools
import math

import jax
import jax.numpy as jnp
from jax import lax
from jax.experimental import pallas as pl
from jax.experimental.pallas import tpu as pltpu
from jax.sharding import PartitionSpec as P

BF = jnp.bfloat16
F32 = jnp.float32
HALO = 16


def dot_nn(a, b):
    return jnp.dot(a, b, preferred_element_type=F32)


def dot_nt(a, b):
    return lax.dot_general(a, b, (((1,), (1,)), ((), ())), preferred_element_type=F32)


def dot_tn(a, b):
    return lax.dot_general(a, b, (((0,), (0,)), ((), ())), preferred_element_type=F32)


def iotas(rows, cols):
    return (
        lax.broadcasted_iota(jnp.int32, (rows, cols), 0),
        lax.broadcasted_iota(jnp.int32, (rows, cols), 1),
    )


def unit_lower_inverse(blocks, size):
    row, col = iotas(size, size)
    diff = row ^ col
    eye = jnp.where(row == col, 1.0, 0.0).astype(F32)
    low = row > col
    inv = [eye - jnp.where(low & (diff < 2), a, 0.0) for a in blocks]
    span = 2
    while span < size:
        pick = low & (diff >= span) & (diff < 2 * span)
        off = [jnp.where(pick, a, 0.0).astype(BF) for a in blocks]
        held = [t.astype(BF) for t in inv]
        step = [dot_nn(h, o).astype(BF) for h, o in zip(held, off)]
        inv = [t - dot_nn(s, h) for t, s, h in zip(inv, step, held)]
        span *= 2
    return inv


def conv_taps(hin, prefix, taps, marks):
    ext = jnp.concatenate([prefix, hin], axis=0)
    shifts = [hin]
    total = hin * taps[0:1, :]
    for lag in range(1, taps.shape[0]):
        moved = pltpu.roll(ext, lag, 0)[HALO:, :]
        moved = jnp.where(marks[:, lag : lag + 1] > 0.0, moved, 0.0)
        shifts.append(moved)
        total = total + moved * taps[lag : lag + 1, :]
    return total, shifts


def prep_kernel(k_ref, h_ref, pre_ref, tap_ref, mark_ref, b_ref, w_ref, t_ref, c_ref, sent_ref):
    length = k_ref.shape[0]
    half = length // 2
    quarter = length // 4
    heads = t_ref.shape[0]
    row, col = iotas(length, length)
    strict = row > col
    total, unused = conv_taps(
        h_ref[...].astype(F32), pre_ref[...].astype(F32), tap_ref[...], mark_ref[...]
    )
    act = total * jax.nn.sigmoid(total)
    houses, blocks, coupled = [], [], []
    for h in range(heads):
        cols = slice(h * 128, (h + 1) * 128)
        a = act[:, cols]
        w = (a * lax.rsqrt(jnp.sum(a * a, axis=1, keepdims=True) + 1e-06)).astype(BF)
        w_ref[:, cols] = w
        houses.append(w)
        full = jnp.where(strict, dot_nt(w, w) * b_ref[:, h * 128 : h * 128 + 1], 0.0)
        coupled.append(full.astype(BF))
        for q in range(4):
            blocks.append(full[q * quarter : (q + 1) * quarter, q * quarter : (q + 1) * quarter])
    inv = unit_lower_inverse(blocks, quarter)
    for h in range(heads):
        cols = slice(h * 128, (h + 1) * 128)
        diag = [t.astype(BF) for t in inv[4 * h : 4 * h + 4]]
        halves = []
        for p in range(2):
            at = p * half
            off = coupled[h][at + quarter : at + half, at : at + quarter]
            corner = -dot_nn(dot_nn(diag[2 * p + 1], off).astype(BF), diag[2 * p])
            zero = jnp.zeros((quarter, quarter), BF)
            halves.append(
                jnp.concatenate(
                    [
                        jnp.concatenate([diag[2 * p], zero], axis=1),
                        jnp.concatenate([corner.astype(BF), diag[2 * p + 1]], axis=1),
                    ],
                    axis=0,
                )
            )
        off = coupled[h][half:, :half]
        corner = -dot_nn(dot_nn(halves[1], off).astype(BF), halves[0])
        t_full = jnp.concatenate(
            [
                jnp.concatenate([halves[0], jnp.zeros((half, half), BF)], axis=1),
                jnp.concatenate([corner.astype(BF), halves[1]], axis=1),
            ],
            axis=0,
        )
        t_ref[h] = t_full
        w = houses[h]
        k = k_ref[:, cols]
        c = jnp.where(strict, dot_nt(w, k) * b_ref[:, h * 128 : h * 128 + 1], 0.0).astype(BF)
        c_ref[h] = c
        z = dot_tn(t_full, w).astype(BF)
        sent_ref[:, cols] = (k.astype(F32) - dot_tn(c, z)).astype(BF)


def attend_kernel(
    q_ref, k_ref, v_ref, w_ref, b_ref, t_ref, c_ref, fk_ref, fv_ref, tc_ref, tr_ref,
    o_ref, p_ref, x_ref, qt_ref,
):
    length = q_ref.shape[0]
    row, col = iotas(length, length)
    causal = row >= col
    q, k, w = q_ref[...], k_ref[...], w_ref[...]
    wb = (w.astype(F32) * b_ref[...]).astype(BF)
    reach = jnp.where(causal, dot_nt(q, w), 0.0).astype(BF)
    x = dot_nn(reach, t_ref[0]).astype(BF)
    x_ref[0] = x
    qt = (q.astype(F32) - dot_nn(x, wb)).astype(BF)
    qt_ref[...] = qt
    scale = 1.0 / math.sqrt(q.shape[1])
    tags = tc_ref[...]
    near = jnp.where(
        causal & (tags == tr_ref[0:1, :]), (dot_nt(q, k) - dot_nn(x, c_ref[0])) * scale, -1e30
    )
    far = jnp.where(tags == tr_ref[1:2, :], dot_nt(qt, fk_ref[...]) * scale, -1e30)
    top = jnp.maximum(
        jnp.max(near, axis=1, keepdims=True), jnp.max(far, axis=1, keepdims=True)
    )
    near = jnp.exp(near - top)
    far = jnp.exp(far - top)
    inv = 1.0 / (jnp.sum(near, axis=1, keepdims=True) + jnp.sum(far, axis=1, keepdims=True))
    near = (near * inv).astype(BF)
    far = (far * inv).astype(BF)
    p_ref[0, :, :length] = near
    p_ref[0, :, length:] = far
    o_ref[...] = (dot_nn(near, v_ref[...]) + dot_nn(far, fv_ref[...])).astype(BF)


def attend_back_kernel(
    g_ref, q_ref, k_ref, v_ref, w_ref, b_ref, t_ref, c_ref, fk_ref, fv_ref, p_ref, x_ref, qt_ref,
    dq_ref, dk_ref, dv_ref, dw_ref, dwb_ref, dfk_ref, dfv_ref,
):
    length = q_ref.shape[0]
    row, col = iotas(length, length)
    q, k, w, g = q_ref[...], k_ref[...], w_ref[...], g_ref[...]
    wb = (w.astype(F32) * b_ref[...]).astype(BF)
    x, t, c = x_ref[0], t_ref[0], c_ref[0]
    near, far = p_ref[0, :, :length], p_ref[0, :, length:]
    dv_ref[...] = dot_tn(near, g)
    dfv_ref[...] = dot_tn(far, g).astype(BF)
    d_near = dot_nt(g, v_ref[...])
    d_far = dot_nt(g, fv_ref[...])
    near, far = near.astype(F32), far.astype(F32)
    mean = jnp.sum(near * d_near, axis=1, keepdims=True) + jnp.sum(
        far * d_far, axis=1, keepdims=True
    )
    scale = 1.0 / math.sqrt(q.shape[1])
    s_near = (near * (d_near - mean) * scale).astype(BF)
    s_far = (far * (d_far - mean) * scale).astype(BF)
    dfk_ref[...] = dot_tn(s_far, qt_ref[...]).astype(BF)
    dqt = dot_nn(s_far, fk_ref[...])
    dqt_low = dqt.astype(BF)
    neg_dx = (dot_nt(s_near, c) + dot_nt(dqt_low, wb)).astype(BF)
    e = jnp.where(row >= col, -dot_nt(neg_dx, t), 0.0).astype(BF)
    dc = jnp.where(row > col, -dot_tn(x, s_near), 0.0).astype(BF)
    da = jnp.where(row > col, -dot_tn(x, e), 0.0).astype(BF)
    dq = dot_nn(
        jnp.concatenate([s_near, s_far, e], axis=1),
        jnp.concatenate([k, fk_ref[...], w], axis=0),
    )
    dq_ref[...] = dq.astype(BF)
    dk_ref[...] = dot_tn(s_near, q) + dot_tn(dc, wb)
    dwb_ref[...] = dot_nn(dc, k) - dot_tn(x, dqt_low) + dot_nn(da, w)
    dw_ref[...] = dot_tn(e, q) + dot_tn(da, wb)


def keys_back_kernel(
    d_ref, bv_ref, q_ref, k_ref, w_ref, b_ref, t_ref, c_ref, h_ref, pre_ref, tap_ref, mark_ref,
    dki_ref, dvi_ref, dwi_ref, dwbi_ref,
    out_ref, tail_ref, dpre_ref, dtap_ref,
):
    length, inner = k_ref.shape
    heads = inner // 128
    row, col = iotas(length, length)
    strict = row > col
    marks = mark_ref[...]
    lanes = lax.broadcasted_iota(jnp.int32, (length, 128), 1)
    side = jnp.zeros((length, 128), F32)
    out_ref[:, :inner] = q_ref[...]
    out_ref[:, 2 * inner : 3 * inner] = (dvi_ref[...] + bv_ref[...].astype(F32)).astype(BF)
    for h in range(heads):
        cols = slice(h * 128, (h + 1) * 128)
        k, w, d, b = k_ref[:, cols], w_ref[:, cols], d_ref[:, cols], b_ref[:, cols]
        wb = (w.astype(F32) * b).astype(BF)
        t, c = t_ref[h], c_ref[h]
        z = dot_tn(t, w).astype(BF)
        dc = jnp.where(strict, -dot_nt(z, d), 0.0).astype(BF)
        f = -dot_nn(t, dot_nn(c, d).astype(BF))
        da = jnp.where(strict, -dot_nt(z, f.astype(BF)), 0.0).astype(BF)
        dk = (dki_ref[:, cols] + d.astype(F32) + dot_tn(dc, wb)).astype(BF)
        out_ref[:, inner + h * 128 : inner + (h + 1) * 128] = dk
        dwb = dwbi_ref[:, cols] + dot_nn(dc, k) + dot_nn(da, w)
        dw = dwi_ref[:, cols] + f + dot_tn(da, wb) + b * dwb
        db = jnp.sum(dwb * w.astype(F32), axis=1, keepdims=True)
        side = jnp.where(lanes == h, db * (b * (1.0 - 0.5 * b)), side)
        taps = tap_ref[:, cols]
        total, shifts = conv_taps(
            h_ref[:, cols].astype(F32), pre_ref[:, cols].astype(F32), taps, marks
        )
        sig = jax.nn.sigmoid(total)
        act = total * sig
        r = lax.rsqrt(jnp.sum(act * act, axis=1, keepdims=True) + 1e-06)
        d_act = r * dw - act * (r * r * r * jnp.sum(act * dw, axis=1, keepdims=True))
        d_total = d_act * sig * (1.0 + total * (1.0 - sig))
        rows = [jnp.sum(d_total * s, axis=0, keepdims=True) for s in shifts]
        dtap_ref[:, cols] = jnp.concatenate(
            rows + [jnp.zeros((8 - len(rows), 128), F32)], axis=0
        )
        pad = jnp.zeros((HALO, 128), F32)
        out = jnp.concatenate([pad, d_total * taps[0:1, :]], axis=0)
        for lag in range(1, taps.shape[0]):
            part = jnp.where(marks[:, lag : lag + 1] > 0.0, d_total, 0.0) * taps[lag : lag + 1, :]
            out = out + pltpu.roll(jnp.concatenate([pad, part], axis=0), length + HALO - lag, 0)
        dpre_ref[:, cols] = out[:HALO, :].astype(BF)
        tail_ref[:, cols] = out[length:, :]
        out_ref[:, 3 * inner + h * 128 : 3 * inner + (h + 1) * 128] = out[HALO:, :].astype(BF)
    out_ref[:, 4 * inner :] = side.astype(BF)


def sds(shape, dtype):
    return jax.ShapeDtypeStruct(shape, dtype)


def cost(micros):
    return pl.CostEstimate(flops=micros * 10**9, bytes_accessed=micros * 10**6, transcendentals=0)


def params():
    return pltpu.CompilerParams(vmem_limit_bytes=56 * 1024 * 1024)


def call_prep(k, hin, prefix, taps, marks, beta):
    length, width = k.shape
    heads = width // 128
    whole = pl.BlockSpec(memory_space=pltpu.VMEM)
    return pl.pallas_call(
        prep_kernel,
        out_shape=(
            sds((length, width), BF),
            sds((heads, length, length), BF),
            sds((heads, length, length), BF),
            sds((length, width), BF),
        ),
        in_specs=[whole] * 6,
        out_specs=[whole] * 4,
        compiler_params=params(),
        cost_estimate=cost(9),
        name="prep",
    )(k, hin, prefix, taps, marks, beta)


def head_specs(length):
    slab = pl.BlockSpec((length, 128), lambda h: (0, h))
    square = pl.BlockSpec((1, length, length), lambda h: (h, 0, 0))
    double = pl.BlockSpec((1, length, 2 * length), lambda h: (h, 0, 0))
    return slab, square, double


def fixed(shape):
    return pl.BlockSpec(shape, lambda h: (0,) * len(shape))


def call_attend(q, k, v, w, beta, t, c, fk, fv, tag_col, tag_rows):
    length, width = q.shape
    heads = width // 128
    slab, square, double = head_specs(length)
    return pl.pallas_call(
        attend_kernel,
        grid=(heads,),
        out_shape=(
            sds((length, width), BF),
            sds((heads, length, 2 * length), BF),
            sds((heads, length, length), BF),
            sds((length, width), BF),
        ),
        in_specs=[slab] * 5
        + [square, square, slab, slab, fixed(tag_col.shape), fixed(tag_rows.shape)],
        out_specs=[slab, double, square, slab],
        compiler_params=params(),
        cost_estimate=cost(11),
        name="attend",
    )(q, k, v, w, beta, t, c, fk, fv, tag_col, tag_rows)


def call_attend_back(g, q, k, v, w, beta, t, c, fk, fv, p, x, qt):
    length, width = q.shape
    heads = width // 128
    slab, square, double = head_specs(length)
    flat = (length, width)
    return pl.pallas_call(
        attend_back_kernel,
        grid=(heads,),
        out_shape=(
            sds(flat, BF), sds(flat, F32), sds(flat, F32), sds(flat, F32), sds(flat, F32),
            sds(flat, BF), sds(flat, BF),
        ),
        in_specs=[slab] * 6 + [square, square, slab, slab, double, square, slab],
        out_specs=[slab] * 7,
        compiler_params=params(),
        cost_estimate=cost(16),
        name="attend_back",
    )(g, q, k, v, w, beta, t, c, fk, fv, p, x, qt)


def call_keys_back(d, back_v, dq, k, w, beta, t, c, hin, prefix, taps, marks, dk, dv, dw, dwb):
    length, width = k.shape
    whole = pl.BlockSpec(memory_space=pltpu.VMEM)
    return pl.pallas_call(
        keys_back_kernel,
        out_shape=(
            sds((length, 4 * width + 128), BF), sds((HALO, width), F32), sds((HALO, width), BF),
            sds((8, width), F32),
        ),
        in_specs=[whole] * 16,
        out_specs=[whole] * 4,
        compiler_params=params(),
        cost_estimate=cost(10),
        name="keys_back",
    )(d, back_v, dq, k, w, beta, t, c, hin, prefix, taps, marks, dk, dv, dw, dwb)


def exchange(mesh_size, name, ident, lhs, rhs, transposed, extras, finish, rows_out, wide_type):
    length = lhs.shape[0]
    model = rhs.shape[0] if transposed else rhs.shape[1]
    n = mesh_size
    chunk = length // n
    many = len(extras)

    def body(*refs):
        lhs_ref, rhs_ref = refs[:2]
        extra_refs = refs[2 : 2 + many]
        out_ref, *row_refs = refs[2 + many : 3 + many + len(rows_out)]
        send, recv, held, send_a, recv_a, send_b, recv_b = refs[3 + many + len(rows_out) :]
        me = lax.axis_index("tensor")
        barrier = pltpu.get_barrier_semaphore()
        peers = [lax.rem(me + i, n) for i in range(1, n)]
        for peer in peers:
            pl.semaphore_signal(
                barrier, inc=1, device_id={"tensor": peer}, device_id_type=pl.DeviceIdType.MESH
            )
        pl.semaphore_wait(barrier, n - 1)

        def rows_of(index):
            return pl.ds(pl.multiple_of(index * chunk, chunk), chunk)

        def partial(index):
            left = lhs_ref[rows_of(index), :]
            return dot_nt(left, rhs_ref[...]) if transposed else dot_nn(left, rhs_ref[...])

        first = []
        for i, peer in enumerate(peers):
            send[i] = partial(peer).astype(BF)
            copy = pltpu.make_async_remote_copy(
                src_ref=send.at[i], dst_ref=recv.at[i],
                send_sem=send_a.at[i], recv_sem=recv_a.at[i],
                device_id={"tensor": peer}, device_id_type=pl.DeviceIdType.MESH,
            )
            copy.start()
            first.append(copy)
        total = partial(me)
        for i, copy in enumerate(first):
            copy.wait()
            total = total + recv[i].astype(F32)
        mine = rows_of(me)
        done, *row_values = finish(total, mine, *extra_refs)
        held[mine, :] = done.astype(BF)
        second = []
        for i, peer in enumerate(peers):
            copy = pltpu.make_async_remote_copy(
                src_ref=held.at[mine, :], dst_ref=held.at[mine, :],
                send_sem=send_b.at[i], recv_sem=recv_b.at[i],
                device_id={"tensor": peer}, device_id_type=pl.DeviceIdType.MESH,
            )
            copy.start()
            second.append(copy)
        for ref, value in zip(row_refs, row_values):
            ref[...] = value
        for copy in second:
            copy.wait()
        out_ref[...] = held[...].astype(wide_type)

    whole = pl.BlockSpec(memory_space=pltpu.VMEM)
    return pl.pallas_call(
        body,
        out_shape=(sds((length, model), wide_type),)
        + tuple(sds((chunk if r is None else r, model), F32) for r in rows_out),
        in_specs=[whole] * (2 + many),
        out_specs=[whole] * (1 + len(rows_out)),
        scratch_shapes=[
            pltpu.VMEM((n - 1, chunk, model), BF),
            pltpu.VMEM((n - 1, chunk, model), BF),
            pltpu.VMEM((length, model), BF),
            pltpu.SemaphoreType.DMA((n - 1,)),
            pltpu.SemaphoreType.DMA((n - 1,)),
            pltpu.SemaphoreType.DMA((n - 1,)),
            pltpu.SemaphoreType.DMA((n - 1,)),
        ],
        compiler_params=pltpu.CompilerParams(
            vmem_limit_bytes=56 * 1024 * 1024, collective_id=ident, has_side_effects=True
        ),
        cost_estimate=cost(40),
        name=name,
    )(lhs, rhs, *extras)


def inverse_rms(x):
    return lax.rsqrt(jnp.mean(x * x, axis=1, keepdims=True) + 1e-06)


def finish_middle(total, mine, tokens_ref, gain_ref):
    middle = tokens_ref[mine, :].astype(F32) + total
    return middle * inverse_rms(middle) * gain_ref[0:1, :], middle


def finish_result(total, mine, middle_ref):
    return (middle_ref[...] + total,)


def norm_back(grad, x, gain):
    r = inverse_rms(x)
    g = grad * gain
    out = r * g - x * (r * r * r * jnp.mean(g * x, axis=1, keepdims=True))
    gain_grad = jnp.sum(grad * x * r, axis=0, keepdims=True)
    return out, jnp.broadcast_to(gain_grad, (8, gain_grad.shape[1]))


def finish_second(total, mine, middle_ref, cot_ref, gain_ref):
    out, gain_grad = norm_back(total, middle_ref[...], gain_ref[0:1, :])
    grad = cot_ref[mine, :].astype(F32) + out
    return grad, grad, gain_grad


def finish_first(total, mine, tokens_ref, grad_ref, gain_ref):
    out, gain_grad = norm_back(total, tokens_ref[mine, :].astype(F32), gain_ref[0:1, :])
    return grad_ref[...] + out, gain_grad


def shift_to(value, axis, steps):
    count = lax.axis_size(axis)
    leading, last = (max(0, -steps), min(count, count - steps))
    return lax.ppermute(value, axis, [(at, at + steps) for at in range(leading, last)])


def own_half(value):
    rows = value.shape[0] // lax.axis_size("context")
    return lax.dynamic_slice_in_dim(value, lax.axis_index("context") * rows, rows, axis=0)


def gather_rows(value):
    return lax.all_gather(own_half(value), ("fsdp", "context"), axis=0, tiled=True)


def gather_cols(value):
    rows, cols = value.shape
    deep, cores = lax.axis_size("fsdp"), lax.axis_size("context")
    parts = lax.all_gather(own_half(value), ("fsdp", "context"), axis=0, tiled=True)
    parts = parts.reshape(deep, rows, cols)
    return jnp.transpose(parts, (1, 0, 2)).reshape(rows, deep * cols)


def scatter_rows(value):
    part = lax.psum_scatter(value, ("fsdp", "context"), scatter_dimension=0, tiled=True)
    return lax.all_gather(part, "context", axis=0, tiled=True)


def depth_major(value):
    rows, cols = value.shape
    deep = lax.axis_size("fsdp")
    parts = jnp.transpose(value.reshape(rows, deep, cols // deep), (1, 0, 2))
    return parts.reshape(deep * rows, cols // deep)


def on_device(
    tokens,
    segments,
    cotangent,
    query_weight,
    key_weight,
    value_weight,
    house_weight,
    beta_weight,
    conv_weight,
    output_weight,
    gate_weight,
    up_weight,
    down_weight,
    first_gain,
    second_gain,
):
    seq_count, length, model = tokens.shape
    rows = first_gain.shape[0]
    deep = lax.axis_size("fsdp")
    inner = query_weight.shape[1]
    heads, tap_count, chans = conv_weight.shape
    assert seq_count == 1 and heads * tap_count * chans == rows
    side = jnp.concatenate(
        [
            beta_weight,
            first_gain[:, None],
            second_gain[:, None],
            conv_weight.reshape(rows, 1),
            jnp.zeros((rows, 128 - heads - 3), BF),
        ],
        axis=1,
    )
    pack = gather_rows(
        jnp.concatenate([query_weight, key_weight, value_weight, house_weight, side], axis=1)
    )
    output_full = gather_cols(output_weight)
    gate_up = gather_rows(jnp.concatenate([gate_weight, up_weight], axis=1))
    down_full = gather_cols(down_weight)
    side_full = pack[:, 4 * inner :]
    gain_one = side_full[:, heads].astype(F32)
    gain_two = side_full[:, heads + 1].astype(F32)
    taps = jnp.transpose(
        side_full[:, heads + 2].reshape(deep, heads, tap_count, chans), (2, 1, 0, 3)
    ).reshape(tap_count, inner).astype(F32)

    tags = (segments[0] + 1).astype(F32)
    far_tags = shift_to(tags, "context", 1)
    near_tags = jnp.concatenate([far_tags[length - tap_count + 1 :], tags])
    marks = jnp.stack(
        [
            near_tags[tap_count - 1 - lag : tap_count - 1 - lag + length] == tags
            for lag in range(tap_count)
        ],
        axis=1,
    ).astype(F32)

    stream = tokens[0].astype(F32)
    scale_one = lax.rsqrt(jnp.mean(stream * stream, axis=1, keepdims=True) + 1e-06)
    normed = (stream * scale_one * gain_one).astype(BF)
    proj = dot_nn(normed, pack[:, : 4 * inner]).astype(BF)
    beta_raw = dot_nn(normed, side_full)[:, :heads]
    beta = jnp.repeat(2.0 * jax.nn.sigmoid(beta_raw), 128, axis=1)
    q, k, v, hin = (proj[:, i * inner : (i + 1) * inner] for i in range(4))
    prefix = shift_to(hin[length - HALO :], "context", 1)
    w, t, c, sent = call_prep(k, hin, prefix, taps, marks, beta)
    far_k = shift_to(sent, "context", 1)
    far_v = shift_to(v, "context", 1)
    mixed, probs, x, qt = call_attend(
        q, k, v, w, beta, t, c, far_k, far_v, tags[:, None], jnp.stack([tags, far_tags])
    )
    n = lax.axis_size("tensor")
    rows_one = jnp.broadcast_to(gain_one[None, :], (8, model))
    rows_two = jnp.broadcast_to(gain_two[None, :], (8, model))
    normed_two, middle = exchange(
        n, "sum_mixed", 1, mixed, output_full, False, (tokens[0], rows_two), finish_middle,
        (None,), BF,
    )

    both = dot_nn(normed_two, gate_up)
    hidden_width = both.shape[1] // 2
    gate, up = both[:, :hidden_width], both[:, hidden_width:]
    sig = jax.nn.sigmoid(gate)
    act = gate * sig
    hidden = (act * up).astype(BF)
    grad_rows = cotangent[0]
    grad_hidden = dot_nt(grad_rows, down_full)
    grad_both = jnp.concatenate(
        [grad_hidden * up * (sig + act * (1.0 - sig)), grad_hidden * act], axis=1
    ).astype(BF)
    grad_down = depth_major(dot_tn(hidden, grad_rows).astype(BF))
    grad_gate_up = dot_tn(normed_two, grad_both).astype(BF)
    grad_both, grad_down, grad_gate_up = lax.optimization_barrier(
        (grad_both, grad_down, grad_gate_up)
    )
    grad_down = scatter_rows(grad_down)
    grad_gate_up = scatter_rows(grad_gate_up)
    grad_attn, grad_middle, grad_second = exchange(
        n, "sum_second", 2, grad_both, gate_up, True, (middle, grad_rows, rows_two),
        finish_second, (None, 8), BF,
    )
    grad_output = depth_major(dot_tn(mixed, grad_attn).astype(BF))
    grad_attn, grad_output, grad_down = lax.optimization_barrier(
        (grad_attn, grad_output, grad_down)
    )
    grad_output = scatter_rows(grad_output)
    grad_mixed = dot_nt(grad_attn, output_full).astype(BF)

    dq, dk, dv, dw, dwb, dfk, dfv = call_attend_back(
        grad_mixed, q, k, v, w, beta, t, c, far_k, far_v, probs, x, qt
    )
    back_k = shift_to(dfk, "context", -1)
    back_v = shift_to(dfv, "context", -1)
    dproj, tail, dpre, dtap = call_keys_back(
        back_k, back_v, dq, k, w, beta, t, c, hin, prefix, taps, marks, dk, dv, dw, dwb
    )
    back_pre = shift_to(dpre, "context", -1).astype(F32)
    dproj = lax.dynamic_update_slice(
        dproj, (tail + back_pre).astype(BF), (length - HALO, 3 * inner)
    )
    dproj, grad_pack = lax.optimization_barrier((dproj, dot_tn(normed, dproj).astype(BF)))
    dproj, grad_gate_up, grad_output = lax.optimization_barrier(
        (dproj, grad_gate_up, grad_output)
    )
    grad_input, grad_first = exchange(
        n, "sum_first", 3, dproj, pack, True, (tokens[0], grad_middle, rows_one),
        finish_first, (8,), F32,
    )
    (result,) = exchange(
        n, "sum_hidden", 4, hidden, down_full, False, (middle,), finish_result, (), BF
    )
    dconv = jnp.transpose(
        dtap[:tap_count].reshape(tap_count, heads, deep, chans), (2, 1, 0, 3)
    ).reshape(model, 1)
    side_cols = lax.broadcasted_iota(jnp.int32, (model, 128), 1)
    side_back = jnp.where(
        side_cols == heads + 2, dconv.astype(BF), grad_pack[:, 4 * inner :]
    )
    shares = scatter_rows(
        jnp.concatenate([grad_pack[:, : 4 * inner], side_back], axis=1)
    ).astype(F32)
    gains = lax.psum(
        jnp.stack([grad_first[0], grad_second[0]]), ("fsdp", "context", "tensor")
    )
    gains = lax.dynamic_slice_in_dim(gains, lax.axis_index("fsdp") * rows, rows, axis=1)
    grad_gate_up = grad_gate_up.astype(F32)
    return (
        result.reshape(tokens.shape),
        grad_input.reshape(tokens.shape),
        shares[:, :inner],
        shares[:, inner : 2 * inner],
        shares[:, 2 * inner : 3 * inner],
        shares[:, 3 * inner : 4 * inner],
        shares[:, 4 * inner : 4 * inner + heads],
        shares[:, 4 * inner + heads + 2].reshape(conv_weight.shape),
        grad_output.astype(F32),
        grad_gate_up[:, :hidden_width],
        grad_gate_up[:, hidden_width:],
        grad_down.astype(F32),
        gains[0],
        gains[1],
    )


def solution(mesh):
    in_specs = (
        P("fsdp", "context", None),
        P("fsdp", "context"),
        P("fsdp", "context", None),
        P("fsdp", "tensor"),
        P("fsdp", "tensor"),
        P("fsdp", "tensor"),
        P("fsdp", "tensor"),
        P("fsdp", "tensor"),
        P("tensor", None, "fsdp"),
        P("tensor", "fsdp"),
        P("fsdp", "tensor"),
        P("fsdp", "tensor"),
        P("tensor", "fsdp"),
        P("fsdp"),
        P("fsdp"),
    )
    out_specs = (
        P("fsdp", "context", None),
        P("fsdp", "context", None),
        P("fsdp", "tensor"),
        P("fsdp", "tensor"),
        P("fsdp", "tensor"),
        P("fsdp", "tensor"),
        P("fsdp", "tensor"),
        P("tensor", None, "fsdp"),
        P("tensor", "fsdp"),
        P("fsdp", "tensor"),
        P("fsdp", "tensor"),
        P("tensor", "fsdp"),
        P("fsdp"),
        P("fsdp"),
    )
    return jax.shard_map(
        on_device, mesh=mesh, in_specs=in_specs, out_specs=out_specs, check_vma=False
    )
```

```python
import functools
import math

import jax
import jax.numpy as jnp
from jax import lax
from jax.experimental import pallas as pl
from jax.experimental.pallas import tpu as pltpu
from jax.sharding import PartitionSpec as P

BF = jnp.bfloat16
F32 = jnp.float32
HALO = 16


def dot_nn(a, b):
    return jnp.dot(a, b, preferred_element_type=F32)


def dot_nt(a, b):
    return lax.dot_general(a, b, (((1,), (1,)), ((), ())), preferred_element_type=F32)


def dot_tn(a, b):
    return lax.dot_general(a, b, (((0,), (0,)), ((), ())), preferred_element_type=F32)


def iotas(rows, cols):
    return (
        lax.broadcasted_iota(jnp.int32, (rows, cols), 0),
        lax.broadcasted_iota(jnp.int32, (rows, cols), 1),
    )


def unit_lower_inverse(blocks, size):
    row, col = iotas(size, size)
    diff = row ^ col
    eye = jnp.where(row == col, 1.0, 0.0).astype(F32)
    low = row > col
    inv = [eye - jnp.where(low & (diff < 2), a, 0.0) for a in blocks]
    span = 2
    while span < size:
        pick = low & (diff >= span) & (diff < 2 * span)
        off = [jnp.where(pick, a, 0.0).astype(BF) for a in blocks]
        held = [t.astype(BF) for t in inv]
        step = [dot_nn(h, o).astype(BF) for h, o in zip(held, off)]
        inv = [t - dot_nn(s, h) for t, s, h in zip(inv, step, held)]
        span *= 2
    return inv


def conv_taps(hin, prefix, taps, marks):
    ext = jnp.concatenate([prefix, hin], axis=0)
    shifts = [hin]
    total = hin * taps[0:1, :]
    for lag in range(1, taps.shape[0]):
        moved = pltpu.roll(ext, lag, 0)[HALO:, :]
        moved = jnp.where(marks[:, lag : lag + 1] > 0.0, moved, 0.0)
        shifts.append(moved)
        total = total + moved * taps[lag : lag + 1, :]
    return total, shifts


def prep_kernel(k_ref, h_ref, pre_ref, tap_ref, mark_ref, b_ref, w_ref, t_ref, c_ref, sent_ref):
    length = k_ref.shape[0]
    half = length // 2
    quarter = length // 4
    heads = t_ref.shape[0]
    row, col = iotas(length, length)
    strict = row > col
    total, unused = conv_taps(
        h_ref[...].astype(F32), pre_ref[...].astype(F32), tap_ref[...], mark_ref[...]
    )
    act = total * jax.nn.sigmoid(total)
    houses, blocks, coupled = [], [], []
    for h in range(heads):
        cols = slice(h * 128, (h + 1) * 128)
        a = act[:, cols]
        w = (a * lax.rsqrt(jnp.sum(a * a, axis=1, keepdims=True) + 1e-06)).astype(BF)
        w_ref[:, cols] = w
        houses.append(w)
        full = jnp.where(strict, dot_nt(w, w) * b_ref[:, h * 128 : h * 128 + 1], 0.0)
        coupled.append(full.astype(BF))
        for q in range(4):
            blocks.append(full[q * quarter : (q + 1) * quarter, q * quarter : (q + 1) * quarter])
    inv = unit_lower_inverse(blocks, quarter)
    for h in range(heads):
        cols = slice(h * 128, (h + 1) * 128)
        diag = [t.astype(BF) for t in inv[4 * h : 4 * h + 4]]
        halves = []
        for p in range(2):
            at = p * half
            off = coupled[h][at + quarter : at + half, at : at + quarter]
            corner = -dot_nn(dot_nn(diag[2 * p + 1], off).astype(BF), diag[2 * p])
            zero = jnp.zeros((quarter, quarter), BF)
            halves.append(
                jnp.concatenate(
                    [
                        jnp.concatenate([diag[2 * p], zero], axis=1),
                        jnp.concatenate([corner.astype(BF), diag[2 * p + 1]], axis=1),
                    ],
                    axis=0,
                )
            )
        off = coupled[h][half:, :half]
        corner = -dot_nn(dot_nn(halves[1], off).astype(BF), halves[0])
        t_full = jnp.concatenate(
            [
                jnp.concatenate([halves[0], jnp.zeros((half, half), BF)], axis=1),
                jnp.concatenate([corner.astype(BF), halves[1]], axis=1),
            ],
            axis=0,
        )
        t_ref[h] = t_full
        w = houses[h]
        k = k_ref[:, cols]
        c = jnp.where(strict, dot_nt(w, k) * b_ref[:, h * 128 : h * 128 + 1], 0.0).astype(BF)
        c_ref[h] = c
        z = dot_tn(t_full, w).astype(BF)
        sent_ref[:, cols] = (k.astype(F32) - dot_tn(c, z)).astype(BF)


def attend_kernel(
    q_ref, k_ref, v_ref, w_ref, b_ref, t_ref, c_ref, fk_ref, fv_ref, tc_ref, tr_ref,
    o_ref, p_ref, x_ref, qt_ref,
):
    length = q_ref.shape[0]
    row, col = iotas(length, length)
    causal = row >= col
    q, k, w = q_ref[...], k_ref[...], w_ref[...]
    wb = (w.astype(F32) * b_ref[...]).astype(BF)
    reach = jnp.where(causal, dot_nt(q, w), 0.0).astype(BF)
    x = dot_nn(reach, t_ref[0]).astype(BF)
    x_ref[0] = x
    qt = (q.astype(F32) - dot_nn(x, wb)).astype(BF)
    qt_ref[...] = qt
    scale = 1.0 / math.sqrt(q.shape[1])
    tags = tc_ref[...]
    near = jnp.where(
        causal & (tags == tr_ref[0:1, :]), (dot_nt(q, k) - dot_nn(x, c_ref[0])) * scale, -1e30
    )
    far = jnp.where(tags == tr_ref[1:2, :], dot_nt(qt, fk_ref[...]) * scale, -1e30)
    top = jnp.maximum(
        jnp.max(near, axis=1, keepdims=True), jnp.max(far, axis=1, keepdims=True)
    )
    near = jnp.exp(near - top)
    far = jnp.exp(far - top)
    inv = 1.0 / (jnp.sum(near, axis=1, keepdims=True) + jnp.sum(far, axis=1, keepdims=True))
    near = (near * inv).astype(BF)
    far = (far * inv).astype(BF)
    p_ref[0, :, :length] = near
    p_ref[0, :, length:] = far
    o_ref[...] = (dot_nn(near, v_ref[...]) + dot_nn(far, fv_ref[...])).astype(BF)


def attend_back_kernel(
    ga_ref, ow_ref, q_ref, k_ref, v_ref, w_ref, b_ref, t_ref, c_ref, fk_ref, fv_ref, p_ref, x_ref,
    qt_ref,
    dq_ref, dk_ref, dv_ref, dw_ref, dwb_ref, dfk_ref, dfv_ref,
):
    length = q_ref.shape[0]
    row, col = iotas(length, length)
    q, k, w = q_ref[...], k_ref[...], w_ref[...]
    g = dot_nn(ga_ref[...], ow_ref[...]).astype(BF)
    wb = (w.astype(F32) * b_ref[...]).astype(BF)
    x, t, c = x_ref[0], t_ref[0], c_ref[0]
    near, far = p_ref[0, :, :length], p_ref[0, :, length:]
    dv_ref[...] = dot_tn(near, g)
    dfv_ref[...] = dot_tn(far, g).astype(BF)
    d_near = dot_nt(g, v_ref[...])
    d_far = dot_nt(g, fv_ref[...])
    near, far = near.astype(F32), far.astype(F32)
    mean = jnp.sum(near * d_near, axis=1, keepdims=True) + jnp.sum(
        far * d_far, axis=1, keepdims=True
    )
    scale = 1.0 / math.sqrt(q.shape[1])
    s_near = (near * (d_near - mean) * scale).astype(BF)
    s_far = (far * (d_far - mean) * scale).astype(BF)
    dfk_ref[...] = dot_tn(s_far, qt_ref[...]).astype(BF)
    dqt = dot_nn(s_far, fk_ref[...])
    dqt_low = dqt.astype(BF)
    neg_dx = (dot_nt(s_near, c) + dot_nt(dqt_low, wb)).astype(BF)
    e = jnp.where(row >= col, -dot_nt(neg_dx, t), 0.0).astype(BF)
    dc = jnp.where(row > col, -dot_tn(x, s_near), 0.0).astype(BF)
    da = jnp.where(row > col, -dot_tn(x, e), 0.0).astype(BF)
    dq = dot_nn(
        jnp.concatenate([s_near, s_far, e], axis=1),
        jnp.concatenate([k, fk_ref[...], w], axis=0),
    )
    dq_ref[...] = dq.astype(BF)
    dk_ref[...] = dot_tn(s_near, q) + dot_tn(dc, wb)
    dwb_ref[...] = dot_nn(dc, k) - dot_tn(x, dqt_low) + dot_nn(da, w)
    dw_ref[...] = dot_tn(e, q) + dot_tn(da, wb)


def keys_back_kernel(
    d_ref, bv_ref, q_ref, k_ref, w_ref, b_ref, t_ref, c_ref, h_ref, pre_ref, tap_ref, mark_ref,
    dki_ref, dvi_ref, dwi_ref, dwbi_ref,
    out_ref, tail_ref, dpre_ref, dtap_ref,
):
    length, inner = k_ref.shape
    heads = inner // 128
    row, col = iotas(length, length)
    strict = row > col
    marks = mark_ref[...]
    lanes = lax.broadcasted_iota(jnp.int32, (length, 128), 1)
    side = jnp.zeros((length, 128), F32)
    out_ref[:, :inner] = q_ref[...]
    out_ref[:, 2 * inner : 3 * inner] = (dvi_ref[...] + bv_ref[...].astype(F32)).astype(BF)
    for h in range(heads):
        cols = slice(h * 128, (h + 1) * 128)
        k, w, d, b = k_ref[:, cols], w_ref[:, cols], d_ref[:, cols], b_ref[:, cols]
        wb = (w.astype(F32) * b).astype(BF)
        t, c = t_ref[h], c_ref[h]
        z = dot_tn(t, w).astype(BF)
        dc = jnp.where(strict, -dot_nt(z, d), 0.0).astype(BF)
        f = -dot_nn(t, dot_nn(c, d).astype(BF))
        da = jnp.where(strict, -dot_nt(z, f.astype(BF)), 0.0).astype(BF)
        dk = (dki_ref[:, cols] + d.astype(F32) + dot_tn(dc, wb)).astype(BF)
        out_ref[:, inner + h * 128 : inner + (h + 1) * 128] = dk
        dwb = dwbi_ref[:, cols] + dot_nn(dc, k) + dot_nn(da, w)
        dw = dwi_ref[:, cols] + f + dot_tn(da, wb) + b * dwb
        db = jnp.sum(dwb * w.astype(F32), axis=1, keepdims=True)
        side = jnp.where(lanes == h, db * (b * (1.0 - 0.5 * b)), side)
        taps = tap_ref[:, cols]
        total, shifts = conv_taps(
            h_ref[:, cols].astype(F32), pre_ref[:, cols].astype(F32), taps, marks
        )
        sig = jax.nn.sigmoid(total)
        act = total * sig
        r = lax.rsqrt(jnp.sum(act * act, axis=1, keepdims=True) + 1e-06)
        d_act = r * dw - act * (r * r * r * jnp.sum(act * dw, axis=1, keepdims=True))
        d_total = d_act * sig * (1.0 + total * (1.0 - sig))
        rows = [jnp.sum(d_total * s, axis=0, keepdims=True) for s in shifts]
        dtap_ref[:, cols] = jnp.concatenate(
            rows + [jnp.zeros((8 - len(rows), 128), F32)], axis=0
        )
        pad = jnp.zeros((HALO, 128), F32)
        out = jnp.concatenate([pad, d_total * taps[0:1, :]], axis=0)
        for lag in range(1, taps.shape[0]):
            part = jnp.where(marks[:, lag : lag + 1] > 0.0, d_total, 0.0) * taps[lag : lag + 1, :]
            out = out + pltpu.roll(jnp.concatenate([pad, part], axis=0), length + HALO - lag, 0)
        dpre_ref[:, cols] = out[:HALO, :].astype(BF)
        tail_ref[:, cols] = out[length:, :]
        out_ref[:, 3 * inner + h * 128 : 3 * inner + (h + 1) * 128] = out[HALO:, :].astype(BF)
    out_ref[:, 4 * inner :] = side.astype(BF)


def sds(shape, dtype):
    return jax.ShapeDtypeStruct(shape, dtype)


def cost(micros):
    return pl.CostEstimate(flops=micros * 10**9, bytes_accessed=micros * 10**6, transcendentals=0)


def params():
    return pltpu.CompilerParams(vmem_limit_bytes=56 * 1024 * 1024)


def call_prep(k, hin, prefix, taps, marks, beta):
    length, width = k.shape
    heads = width // 128
    whole = pl.BlockSpec(memory_space=pltpu.VMEM)
    return pl.pallas_call(
        prep_kernel,
        out_shape=(
            sds((length, width), BF),
            sds((heads, length, length), BF),
            sds((heads, length, length), BF),
            sds((length, width), BF),
        ),
        in_specs=[whole] * 6,
        out_specs=[whole] * 4,
        compiler_params=params(),
        cost_estimate=cost(9),
        name="prep",
    )(k, hin, prefix, taps, marks, beta)


def head_specs(length):
    slab = pl.BlockSpec((length, 128), lambda h: (0, h))
    square = pl.BlockSpec((1, length, length), lambda h: (h, 0, 0))
    double = pl.BlockSpec((1, length, 2 * length), lambda h: (h, 0, 0))
    return slab, square, double


def fixed(shape):
    return pl.BlockSpec(shape, lambda h: (0,) * len(shape))


def call_attend(q, k, v, w, beta, t, c, fk, fv, tag_col, tag_rows):
    length, width = q.shape
    heads = width // 128
    slab, square, double = head_specs(length)
    return pl.pallas_call(
        attend_kernel,
        grid=(heads,),
        out_shape=(
            sds((length, width), BF),
            sds((heads, length, 2 * length), BF),
            sds((heads, length, length), BF),
            sds((length, width), BF),
        ),
        in_specs=[slab] * 5
        + [square, square, slab, slab, fixed(tag_col.shape), fixed(tag_rows.shape)],
        out_specs=[slab, double, square, slab],
        compiler_params=params(),
        cost_estimate=cost(11),
        name="attend",
    )(q, k, v, w, beta, t, c, fk, fv, tag_col, tag_rows)


def call_attend_back(ga, ow, q, k, v, w, beta, t, c, fk, fv, p, x, qt):
    length, width = q.shape
    heads = width // 128
    slab, square, double = head_specs(length)
    flat = (length, width)
    return pl.pallas_call(
        attend_back_kernel,
        grid=(heads,),
        out_shape=(
            sds(flat, BF), sds(flat, F32), sds(flat, F32), sds(flat, F32), sds(flat, F32),
            sds(flat, BF), sds(flat, BF),
        ),
        in_specs=[fixed(ga.shape), pl.BlockSpec((ow.shape[0], 128), lambda h: (0, h))]
        + [slab] * 5
        + [square, square, slab, slab, double, square, slab],
        out_specs=[slab] * 7,
        compiler_params=params(),
        cost_estimate=cost(16),
        name="attend_back",
    )(ga, ow, q, k, v, w, beta, t, c, fk, fv, p, x, qt)


def call_keys_back(d, back_v, dq, k, w, beta, t, c, hin, prefix, taps, marks, dk, dv, dw, dwb):
    length, width = k.shape
    whole = pl.BlockSpec(memory_space=pltpu.VMEM)
    return pl.pallas_call(
        keys_back_kernel,
        out_shape=(
            sds((length, 4 * width + 128), BF), sds((HALO, width), F32), sds((HALO, width), BF),
            sds((8, width), F32),
        ),
        in_specs=[whole] * 16,
        out_specs=[whole] * 4,
        compiler_params=params(),
        cost_estimate=cost(10),
        name="keys_back",
    )(d, back_v, dq, k, w, beta, t, c, hin, prefix, taps, marks, dk, dv, dw, dwb)


def exchange(n, name, ident, product, operands, specs, extras, finish, rows_out, wide_type, share):
    length, model = operands[0].shape[0], operands[1].shape[0]
    chunk = length // n
    given = len(operands)
    many = len(extras)

    def body(*refs):
        operand_refs = refs[:given]
        extra_refs = refs[given : given + many]
        last = given + many + 1 + len(rows_out)
        out_ref, *row_refs = refs[given + many : last]
        send, recv, held, send_a, recv_a, send_b, recv_b, *small = refs[last:]
        me = lax.axis_index("tensor")
        barrier = pltpu.get_barrier_semaphore()
        peers = [lax.rem(me + i, n) for i in range(1, n)]
        for peer in peers:
            pl.semaphore_signal(
                barrier, inc=1, device_id={"tensor": peer}, device_id_type=pl.DeviceIdType.MESH
            )
        pl.semaphore_wait(barrier, n - 1)

        def rows_of(index):
            return pl.ds(pl.multiple_of(index * chunk, chunk), chunk)

        def partial(index):
            return product(rows_of(index), *operand_refs)

        first = []
        for i, peer in enumerate(peers):
            send[i] = partial(peer).astype(BF)
            copy = pltpu.make_async_remote_copy(
                src_ref=send.at[i], dst_ref=recv.at[i],
                send_sem=send_a.at[i], recv_sem=recv_a.at[i],
                device_id={"tensor": peer}, device_id_type=pl.DeviceIdType.MESH,
            )
            copy.start()
            first.append(copy)
        total = partial(me)
        for i, copy in enumerate(first):
            copy.wait()
            total = total + recv[i].astype(F32)
        mine = rows_of(me)
        done, *row_values = finish(total, mine, *extra_refs)
        held[mine, :] = done.astype(BF)
        second = []
        for i, peer in enumerate(peers):
            copy = pltpu.make_async_remote_copy(
                src_ref=held.at[mine, :], dst_ref=held.at[mine, :],
                send_sem=send_b.at[i], recv_sem=recv_b.at[i],
                device_id={"tensor": peer}, device_id_type=pl.DeviceIdType.MESH,
            )
            copy.start()
            second.append(copy)
        if share:
            mine_small, slots, send_c, recv_c = small
            mine_small[...] = row_values[-1]
            slots[me] = row_values[-1]
            third = []
            for i, peer in enumerate(peers):
                copy = pltpu.make_async_remote_copy(
                    src_ref=mine_small, dst_ref=slots.at[me],
                    send_sem=send_c.at[i], recv_sem=recv_c.at[i],
                    device_id={"tensor": peer}, device_id_type=pl.DeviceIdType.MESH,
                )
                copy.start()
                third.append(copy)
        for ref, value in zip(row_refs, row_values):
            ref[...] = value
        if share:
            for copy in third:
                copy.wait()
            row_refs[-1][...] = sum(slots[i] for i in range(n))
        for copy in second:
            copy.wait()
        out_ref[...] = held[...].astype(wide_type)

    whole = pl.BlockSpec(memory_space=pltpu.VMEM)
    return pl.pallas_call(
        body,
        out_shape=(sds((length, model), wide_type),)
        + tuple(sds((chunk if r is None else r, model), F32) for r in rows_out),
        in_specs=[whole if spec is None else spec for spec in specs] + [whole] * many,
        out_specs=[whole] * (1 + len(rows_out)),
        scratch_shapes=[
            pltpu.VMEM((n - 1, chunk, model), BF),
            pltpu.VMEM((n - 1, chunk, model), BF),
            pltpu.VMEM((length, model), BF),
            pltpu.SemaphoreType.DMA((n - 1,)),
            pltpu.SemaphoreType.DMA((n - 1,)),
            pltpu.SemaphoreType.DMA((n - 1,)),
            pltpu.SemaphoreType.DMA((n - 1,)),
        ]
        + (
            [
                pltpu.VMEM((8, model), F32),
                pltpu.VMEM((n, 8, model), F32),
                pltpu.SemaphoreType.DMA((n - 1,)),
                pltpu.SemaphoreType.DMA((n - 1,)),
            ]
            if share
            else []
        ),
        compiler_params=pltpu.CompilerParams(
            vmem_limit_bytes=56 * 1024 * 1024, collective_id=ident, has_side_effects=True
        ),
        cost_estimate=cost(40),
        name=name,
    )(*operands, *extras)


def inverse_rms(x):
    return lax.rsqrt(jnp.mean(x * x, axis=1, keepdims=True) + 1e-06)


def finish_middle(total, mine, tokens_ref, gain_ref):
    middle = tokens_ref[mine, :].astype(F32) + total
    return middle * inverse_rms(middle) * gain_ref[0:1, :], middle


def finish_result(total, mine, middle_ref):
    return (middle_ref[...] + total,)


def norm_back(grad, x, gain):
    r = inverse_rms(x)
    g = grad * gain
    out = r * g - x * (r * r * r * jnp.mean(g * x, axis=1, keepdims=True))
    gain_grad = jnp.sum(grad * x * r, axis=0, keepdims=True)
    return out, jnp.broadcast_to(gain_grad, (8, gain_grad.shape[1]))


def finish_second(total, mine, middle_ref, cot_ref, gain_ref):
    out, gain_grad = norm_back(total, middle_ref[...], gain_ref[0:1, :])
    grad = cot_ref[mine, :].astype(F32) + out
    return grad, grad, gain_grad


def finish_first(total, mine, tokens_ref, grad_ref, gain_ref, second_ref):
    out, gain_grad = norm_back(total, tokens_ref[mine, :].astype(F32), gain_ref[0:1, :])
    row = lax.broadcasted_iota(jnp.int32, gain_grad.shape, 0)
    return grad_ref[...] + out, jnp.where(row == 0, gain_grad, second_ref[...])


def plain_nt(rows, lhs_ref, rhs_ref):
    return dot_nt(lhs_ref[rows, :], rhs_ref[...])


def blocks_nt(width, offset, stride):
    def product(rows, lhs_ref, rhs_ref):
        total = None
        for j in range(lhs_ref.shape[1] // width):
            at = j * stride + offset
            term = dot_nt(lhs_ref[rows, j * width : (j + 1) * width], rhs_ref[:, at : at + width])
            total = term if total is None else total + term
        return total

    return product


def gains_kernel(deep, cores, x_ref, out_ref, slots, send_sem, recv_sem):
    z, core = lax.axis_index("fsdp"), lax.axis_index("context")
    me = z * cores + core
    count = deep * cores
    barrier = pltpu.get_barrier_semaphore()
    peers = []
    for i in range(1, count):
        peer = lax.rem(me + i, count)
        peers.append({"fsdp": peer // cores, "context": lax.rem(peer, cores)})
    for peer in peers:
        pl.semaphore_signal(barrier, inc=1, device_id=peer, device_id_type=pl.DeviceIdType.MESH)
    pl.semaphore_wait(barrier, count - 1)
    copies = []
    for i, peer in enumerate(peers):
        copy = pltpu.make_async_remote_copy(
            src_ref=x_ref.at[peer["fsdp"]], dst_ref=slots.at[me],
            send_sem=send_sem.at[i], recv_sem=recv_sem.at[i],
            device_id=peer, device_id_type=pl.DeviceIdType.MESH,
        )
        copy.start()
        copies.append(copy)
    slots[me] = x_ref[z]
    for copy in copies:
        copy.wait()
    out_ref[...] = sum(slots[i] for i in range(count))


def call_gains(x, cores):
    deep, eight, rows = x.shape
    count = deep * cores
    whole = pl.BlockSpec(memory_space=pltpu.VMEM)
    return pl.pallas_call(
        functools.partial(gains_kernel, deep, cores),
        out_shape=sds((eight, rows), F32),
        in_specs=[whole],
        out_specs=whole,
        scratch_shapes=[
            pltpu.VMEM((count, eight, rows), F32),
            pltpu.SemaphoreType.DMA((count - 1,)),
            pltpu.SemaphoreType.DMA((count - 1,)),
        ],
        compiler_params=pltpu.CompilerParams(collective_id=5, has_side_effects=True),
        cost_estimate=cost(6),
        name="sum_gains",
    )(x)


def ffn_kernel(n_ref, cot_ref, w_ref, hid_ref, gb_ref, gw_ref, nt, ct):
    width = hid_ref.shape[1]

    @pl.when(pl.program_id(0) == 0)
    def turn():
        nt[...] = n_ref[...].T
        ct[...] = cot_ref[...].T

    both = dot_nn(n_ref[...], w_ref[:, : 2 * width])
    gate, up = both[:, :width], both[:, width:]
    back = dot_nn(cot_ref[...], w_ref[:, 2 * width :])
    sig = jax.nn.sigmoid(gate)
    act = gate * sig
    hidden = (act * up).astype(BF)
    hid_ref[...] = hidden
    grad = jnp.concatenate(
        [(back * up * (sig + act * (1.0 - sig))).astype(BF), (back * act).astype(BF)], axis=1
    )
    gb_ref[...] = grad
    gw_ref[:, : 2 * width] = dot_nn(nt[...], grad).astype(BF)
    gw_ref[:, 2 * width :] = dot_nn(ct[...], hidden).astype(BF)


def call_ffn(normed, cot, weights, width):
    length, model = normed.shape
    steps = weights.shape[1] // (3 * width)
    return pl.pallas_call(
        ffn_kernel,
        grid=(steps,),
        out_shape=(
            sds((length, steps * width), BF),
            sds((length, steps * 2 * width), BF),
            sds(weights.shape, BF),
        ),
        in_specs=[
            fixed(normed.shape), fixed(cot.shape),
            pl.BlockSpec((model, 3 * width), lambda j: (0, j)),
        ],
        out_specs=[
            pl.BlockSpec((length, width), lambda j: (0, j)),
            pl.BlockSpec((length, 2 * width), lambda j: (0, j)),
            pl.BlockSpec((model, 3 * width), lambda j: (0, j)),
        ],
        scratch_shapes=[pltpu.VMEM((model, length), BF), pltpu.VMEM((model, length), BF)],
        compiler_params=params(),
        cost_estimate=cost(14),
        name="ffn",
    )(normed, cot, weights)


def grads_kernel(lane, n_ref, ga_ref, d_ref, m_ref, conv_ref, out_ref):
    wide = d_ref.shape[1]
    main = wide - 128
    out_ref[:, :main] = dot_tn(n_ref[...], d_ref[:, :main]).astype(BF)
    side = dot_tn(n_ref[...], d_ref[:, main:])
    lanes = lax.broadcasted_iota(jnp.int32, side.shape, 1)
    out_ref[:, main:wide] = jnp.where(lanes == lane, conv_ref[...], side).astype(BF)
    out_ref[:, wide:] = dot_tn(ga_ref[...], m_ref[...]).astype(BF)


def call_grads(lane, normed, ga, dproj, mixed, dconv):
    length, model = normed.shape
    block = 384
    wide = dproj.shape[1] + mixed.shape[1]
    part = pl.BlockSpec((length, block), lambda i: (0, i))
    return pl.pallas_call(
        functools.partial(grads_kernel, lane),
        grid=(model // block,),
        out_shape=sds((model, wide), BF),
        in_specs=[
            part, part, fixed(dproj.shape), fixed(mixed.shape),
            pl.BlockSpec((block, 1), lambda i: (i, 0)),
        ],
        out_specs=pl.BlockSpec((block, wide), lambda i: (i, 0)),
        compiler_params=params(),
        cost_estimate=cost(7),
        name="grads",
    )(normed, ga, dproj, mixed, dconv)


def shift_to(value, axis, steps):
    count = lax.axis_size(axis)
    leading, last = (max(0, -steps), min(count, count - steps))
    return lax.ppermute(value, axis, [(at, at + steps) for at in range(leading, last)])


def own_half(value):
    rows = value.shape[0] // lax.axis_size("context")
    return lax.dynamic_slice_in_dim(value, lax.axis_index("context") * rows, rows, axis=0)


def gather_rows(value):
    return lax.all_gather(own_half(value), ("fsdp", "context"), axis=0, tiled=True)


def scatter_half(value):
    return lax.psum_scatter(value, ("fsdp", "context"), scatter_dimension=0, tiled=True)


def both_halves(value):
    return lax.all_gather(value, "context", axis=0, tiled=True)


FBLOCK = 256


def on_device(
    tokens,
    segments,
    cotangent,
    query_weight,
    key_weight,
    value_weight,
    house_weight,
    beta_weight,
    conv_weight,
    output_weight,
    gate_weight,
    up_weight,
    down_weight,
    first_gain,
    second_gain,
):
    seq_count, length, model = tokens.shape
    rows = first_gain.shape[0]
    deep = lax.axis_size("fsdp")
    inner = query_weight.shape[1]
    heads, tap_count, chans = conv_weight.shape
    assert seq_count == 1 and heads * tap_count * chans == rows
    side = jnp.concatenate(
        [
            beta_weight,
            first_gain[:, None],
            second_gain[:, None],
            conv_weight.reshape(rows, 1),
            jnp.zeros((rows, 128 - heads - 3), BF),
        ],
        axis=1,
    )
    pack = gather_rows(
        jnp.concatenate([query_weight, key_weight, value_weight, house_weight, side], axis=1)
    )
    out_t = gather_rows(output_weight.T)
    hidden_width = gate_weight.shape[1]
    steps = hidden_width // FBLOCK
    down_t = down_weight.T
    ffn_w = gather_rows(
        jnp.concatenate(
            [
                part[:, j * FBLOCK : (j + 1) * FBLOCK]
                for j in range(steps)
                for part in (gate_weight, up_weight, down_t)
            ],
            axis=1,
        )
    )
    side_full = pack[:, 4 * inner :]
    gain_one = side_full[:, heads].astype(F32)
    gain_two = side_full[:, heads + 1].astype(F32)
    taps = jnp.transpose(
        side_full[:, heads + 2].reshape(deep, heads, tap_count, chans), (2, 1, 0, 3)
    ).reshape(tap_count, inner).astype(F32)

    tags = (segments[0] + 1).astype(F32)
    far_tags = shift_to(tags, "context", 1)
    near_tags = jnp.concatenate([far_tags[length - tap_count + 1 :], tags])
    marks = jnp.stack(
        [
            near_tags[tap_count - 1 - lag : tap_count - 1 - lag + length] == tags
            for lag in range(tap_count)
        ],
        axis=1,
    ).astype(F32)

    stream = tokens[0].astype(F32)
    scale_one = lax.rsqrt(jnp.mean(stream * stream, axis=1, keepdims=True) + 1e-06)
    normed = (stream * scale_one * gain_one).astype(BF)
    proj = dot_nn(normed, pack[:, : 4 * inner]).astype(BF)
    beta_raw = dot_nn(normed, side_full)[:, :heads]
    beta = jnp.repeat(2.0 * jax.nn.sigmoid(beta_raw), 128, axis=1)
    q, k, v, hin = (proj[:, i * inner : (i + 1) * inner] for i in range(4))
    prefix = shift_to(hin[length - HALO :], "context", 1)
    w, t, c, sent = call_prep(k, hin, prefix, taps, marks, beta)
    far_k = shift_to(sent, "context", 1)
    far_v = shift_to(v, "context", 1)
    mixed, probs, x, qt = call_attend(
        q, k, v, w, beta, t, c, far_k, far_v, tags[:, None], jnp.stack([tags, far_tags])
    )
    n = lax.axis_size("tensor")
    rows_one = jnp.broadcast_to(gain_one[None, :], (8, model))
    rows_two = jnp.broadcast_to(gain_two[None, :], (8, model))
    normed_two, middle = exchange(
        n, "sum_mixed", 1, plain_nt, (mixed, out_t), (None, None), (tokens[0], rows_two),
        finish_middle, (None,), BF, False,
    )
    cot = cotangent[0]
    hidden, grad_both, grad_ffn = call_ffn(normed_two, cot, ffn_w, FBLOCK)
    grad_both, grad_ffn = lax.optimization_barrier((grad_both, grad_ffn))
    grad_ffn = scatter_half(grad_ffn)
    grad_attn, grad_middle, grad_second = exchange(
        n, "sum_second", 2, blocks_nt(2 * FBLOCK, 0, 3 * FBLOCK), (grad_both, ffn_w),
        (None, None), (middle, cot, rows_two), finish_second, (None, 8), BF, False,
    )

    dq, dk, dv, dw, dwb, dfk, dfv = call_attend_back(
        grad_attn, out_t, q, k, v, w, beta, t, c, far_k, far_v, probs, x, qt
    )
    back_k = shift_to(dfk, "context", -1)
    back_v = shift_to(dfv, "context", -1)
    dproj, tail, dpre, dtap = call_keys_back(
        back_k, back_v, dq, k, w, beta, t, c, hin, prefix, taps, marks, dk, dv, dw, dwb
    )
    back_pre = shift_to(dpre, "context", -1).astype(F32)
    dproj = lax.dynamic_update_slice(
        dproj, (tail + back_pre).astype(BF), (length - HALO, 3 * inner)
    )
    dconv = jnp.transpose(
        dtap[:tap_count].reshape(tap_count, heads, deep, chans), (2, 1, 0, 3)
    ).reshape(model, 1)
    grad_pack = call_grads(heads + 2, normed, grad_attn, dproj, mixed, dconv)
    dproj, grad_pack, grad_ffn = lax.optimization_barrier((dproj, grad_pack, grad_ffn))
    grad_pack = scatter_half(grad_pack)
    grad_input, gains = exchange(
        n, "sum_first", 3, plain_nt, (dproj, pack), (None, None),
        (tokens[0], grad_middle, rows_one, grad_second), finish_first, (8,), F32, True,
    )
    gains = jnp.transpose(gains.reshape(8, deep, rows), (1, 0, 2))
    gains = call_gains(gains, lax.axis_size("context"))
    hidden, gains = lax.optimization_barrier((hidden, gains))
    (result,) = exchange(
        n, "sum_hidden", 4, blocks_nt(FBLOCK, 2 * FBLOCK, 3 * FBLOCK), (hidden, ffn_w),
        (None, None), (middle,), finish_result, (), BF, False,
    )
    result, grad_pack = lax.optimization_barrier((result, grad_pack))
    blocks = both_halves(grad_ffn).astype(F32).reshape(rows, steps, 3, FBLOCK)
    gate_grad, up_grad, down_grad = (
        blocks[:, :, i].reshape(rows, hidden_width) for i in range(3)
    )
    shares = both_halves(grad_pack).astype(F32)
    return (
        result.reshape(tokens.shape),
        grad_input.reshape(tokens.shape),
        shares[:, :inner],
        shares[:, inner : 2 * inner],
        shares[:, 2 * inner : 3 * inner],
        shares[:, 3 * inner : 4 * inner],
        shares[:, 4 * inner : 4 * inner + heads],
        shares[:, 4 * inner + heads + 2].reshape(conv_weight.shape),
        shares[:, 4 * inner + 128 :].T,
        gate_grad,
        up_grad,
        down_grad.T,
        gains[0],
        gains[1],
    )


def solution(mesh):
    in_specs = (
        P("fsdp", "context", None),
        P("fsdp", "context"),
        P("fsdp", "context", None),
        P("fsdp", "tensor"),
        P("fsdp", "tensor"),
        P("fsdp", "tensor"),
        P("fsdp", "tensor"),
        P("fsdp", "tensor"),
        P("tensor", None, "fsdp"),
        P("tensor", "fsdp"),
        P("fsdp", "tensor"),
        P("fsdp", "tensor"),
        P("tensor", "fsdp"),
        P("fsdp"),
        P("fsdp"),
    )
    out_specs = (
        P("fsdp", "context", None),
        P("fsdp", "context", None),
        P("fsdp", "tensor"),
        P("fsdp", "tensor"),
        P("fsdp", "tensor"),
        P("fsdp", "tensor"),
        P("fsdp", "tensor"),
        P("tensor", None, "fsdp"),
        P("tensor", "fsdp"),
        P("fsdp", "tensor"),
        P("fsdp", "tensor"),
        P("tensor", "fsdp"),
        P("fsdp"),
        P("fsdp"),
    )
    return jax.shard_map(
        on_device, mesh=mesh, in_specs=in_specs, out_specs=out_specs, check_vma=False
    )
```

```python
import functools
import math

import jax
import jax.numpy as jnp
from jax import lax
from jax.experimental import pallas as pl
from jax.experimental.pallas import tpu as pltpu
from jax.sharding import PartitionSpec as P

BF = jnp.bfloat16
F32 = jnp.float32
HALO = 16


def dot_nn(a, b):
    return jnp.dot(a, b, preferred_element_type=F32)


def dot_nt(a, b):
    return lax.dot_general(a, b, (((1,), (1,)), ((), ())), preferred_element_type=F32)


def dot_tn(a, b):
    return lax.dot_general(a, b, (((0,), (0,)), ((), ())), preferred_element_type=F32)


def iotas(rows, cols):
    return (
        lax.broadcasted_iota(jnp.int32, (rows, cols), 0),
        lax.broadcasted_iota(jnp.int32, (rows, cols), 1),
    )


def unit_lower_inverse(blocks, size):
    row, col = iotas(size, size)
    diff = row ^ col
    eye = jnp.where(row == col, 1.0, 0.0).astype(F32)
    low = row > col
    inv = [eye - jnp.where(low & (diff < 2), a, 0.0) for a in blocks]
    span = 2
    while span < size:
        pick = low & (diff >= span) & (diff < 2 * span)
        off = [jnp.where(pick, a, 0.0).astype(BF) for a in blocks]
        held = [t.astype(BF) for t in inv]
        step = [dot_nn(h, o).astype(BF) for h, o in zip(held, off)]
        inv = [t - dot_nn(s, h) for t, s, h in zip(inv, step, held)]
        span *= 2
    return inv


def conv_taps(hin, prefix, taps, marks):
    ext = jnp.concatenate([prefix, hin], axis=0)
    shifts = [hin]
    total = hin * taps[0:1, :]
    for lag in range(1, taps.shape[0]):
        moved = pltpu.roll(ext, lag, 0)[HALO:, :]
        moved = jnp.where(marks[:, lag : lag + 1] > 0.0, moved, 0.0)
        shifts.append(moved)
        total = total + moved * taps[lag : lag + 1, :]
    return total, shifts


def prep_kernel(k_ref, h_ref, pre_ref, tap_ref, mark_ref, b_ref, w_ref, t_ref, c_ref, sent_ref):
    length = k_ref.shape[0]
    half = length // 2
    quarter = length // 4
    heads = t_ref.shape[0]
    row, col = iotas(length, length)
    strict = row > col
    total, unused = conv_taps(
        h_ref[...].astype(F32), pre_ref[...].astype(F32), tap_ref[...], mark_ref[...]
    )
    act = total * jax.nn.sigmoid(total)
    houses, blocks, coupled = [], [], []
    for h in range(heads):
        cols = slice(h * 128, (h + 1) * 128)
        a = act[:, cols]
        w = (a * lax.rsqrt(jnp.sum(a * a, axis=1, keepdims=True) + 1e-06)).astype(BF)
        w_ref[:, cols] = w
        houses.append(w)
        full = jnp.where(strict, dot_nt(w, w) * b_ref[:, h * 128 : h * 128 + 1], 0.0)
        coupled.append(full.astype(BF))
        for q in range(4):
            blocks.append(full[q * quarter : (q + 1) * quarter, q * quarter : (q + 1) * quarter])
    inv = unit_lower_inverse(blocks, quarter)
    for h in range(heads):
        cols = slice(h * 128, (h + 1) * 128)
        diag = [t.astype(BF) for t in inv[4 * h : 4 * h + 4]]
        halves = []
        for p in range(2):
            at = p * half
            off = coupled[h][at + quarter : at + half, at : at + quarter]
            corner = -dot_nn(dot_nn(diag[2 * p + 1], off).astype(BF), diag[2 * p])
            zero = jnp.zeros((quarter, quarter), BF)
            halves.append(
                jnp.concatenate(
                    [
                        jnp.concatenate([diag[2 * p], zero], axis=1),
                        jnp.concatenate([corner.astype(BF), diag[2 * p + 1]], axis=1),
                    ],
                    axis=0,
                )
            )
        off = coupled[h][half:, :half]
        corner = -dot_nn(dot_nn(halves[1], off).astype(BF), halves[0])
        t_full = jnp.concatenate(
            [
                jnp.concatenate([halves[0], jnp.zeros((half, half), BF)], axis=1),
                jnp.concatenate([corner.astype(BF), halves[1]], axis=1),
            ],
            axis=0,
        )
        t_ref[h] = t_full
        w = houses[h]
        k = k_ref[:, cols]
        c = jnp.where(strict, dot_nt(w, k) * b_ref[:, h * 128 : h * 128 + 1], 0.0).astype(BF)
        c_ref[h] = c
        z = dot_tn(t_full, w).astype(BF)
        sent_ref[:, cols] = (k.astype(F32) - dot_tn(c, z)).astype(BF)


def attend_kernel(
    q_ref, k_ref, v_ref, w_ref, b_ref, t_ref, c_ref, fk_ref, fv_ref, tc_ref, tr_ref,
    o_ref, p_ref, x_ref, qt_ref,
):
    length = q_ref.shape[0]
    row, col = iotas(length, length)
    causal = row >= col
    q, k, w = q_ref[...], k_ref[...], w_ref[...]
    wb = (w.astype(F32) * b_ref[...]).astype(BF)
    reach = jnp.where(causal, dot_nt(q, w), 0.0).astype(BF)
    x = dot_nn(reach, t_ref[0]).astype(BF)
    x_ref[0] = x
    qt = (q.astype(F32) - dot_nn(x, wb)).astype(BF)
    qt_ref[...] = qt
    scale = 1.0 / math.sqrt(q.shape[1])
    tags = tc_ref[...]
    near = jnp.where(
        causal & (tags == tr_ref[0:1, :]), (dot_nt(q, k) - dot_nn(x, c_ref[0])) * scale, -1e30
    )
    far = jnp.where(tags == tr_ref[1:2, :], dot_nt(qt, fk_ref[...]) * scale, -1e30)
    top = jnp.maximum(
        jnp.max(near, axis=1, keepdims=True), jnp.max(far, axis=1, keepdims=True)
    )
    near = jnp.exp(near - top)
    far = jnp.exp(far - top)
    inv = 1.0 / (jnp.sum(near, axis=1, keepdims=True) + jnp.sum(far, axis=1, keepdims=True))
    near = (near * inv).astype(BF)
    far = (far * inv).astype(BF)
    p_ref[0, :, :length] = near
    p_ref[0, :, length:] = far
    o_ref[...] = (dot_nn(near, v_ref[...]) + dot_nn(far, fv_ref[...])).astype(BF)


def attend_back_kernel(
    n, part_ref, mid_ref, ga_ref, ow_ref, q_ref, k_ref, v_ref, w_ref, b_ref, t_ref, c_ref, fk_ref, fv_ref, p_ref, x_ref,
    qt_ref,
    dq_ref, dk_ref, dv_ref, dw_ref, dwb_ref, dfk_ref, dfv_ref, res_ref,
    own, recv, own_sem, send_sem, recv_sem,
):
    length = q_ref.shape[0]
    chunk = length // n
    me = lax.axis_index("tensor")

    def rows_of(index):
        return pl.ds(pl.multiple_of(index * chunk, chunk), chunk)

    def moves():
        out = [pltpu.make_async_copy(part_ref.at[rows_of(me), :], own, own_sem)]
        for i in range(1, n):
            peer = lax.rem(me + i, n)
            out.append(
                pltpu.make_async_remote_copy(
                    src_ref=part_ref.at[rows_of(peer), :], dst_ref=recv.at[i - 1],
                    send_sem=send_sem.at[i - 1], recv_sem=recv_sem.at[i - 1],
                    device_id={"tensor": peer}, device_id_type=pl.DeviceIdType.MESH,
                )
            )
        return out

    @pl.when(pl.program_id(0) == 0)
    def begin():
        barrier = pltpu.get_barrier_semaphore()
        for i in range(1, n):
            pl.semaphore_signal(
                barrier, inc=1, device_id={"tensor": lax.rem(me + i, n)},
                device_id_type=pl.DeviceIdType.MESH,
            )
        pl.semaphore_wait(barrier, n - 1)
        for copy in moves():
            copy.start()

    row, col = iotas(length, length)
    q, k, w = q_ref[...], k_ref[...], w_ref[...]
    g = dot_nn(ga_ref[...], ow_ref[...]).astype(BF)
    wb = (w.astype(F32) * b_ref[...]).astype(BF)
    x, t, c = x_ref[0], t_ref[0], c_ref[0]
    near, far = p_ref[0, :, :length], p_ref[0, :, length:]
    dv_ref[...] = dot_tn(near, g)
    dfv_ref[...] = dot_tn(far, g).astype(BF)
    d_near = dot_nt(g, v_ref[...])
    d_far = dot_nt(g, fv_ref[...])
    near, far = near.astype(F32), far.astype(F32)
    mean = jnp.sum(near * d_near, axis=1, keepdims=True) + jnp.sum(
        far * d_far, axis=1, keepdims=True
    )
    scale = 1.0 / math.sqrt(q.shape[1])
    s_near = (near * (d_near - mean) * scale).astype(BF)
    s_far = (far * (d_far - mean) * scale).astype(BF)
    dfk_ref[...] = dot_tn(s_far, qt_ref[...]).astype(BF)
    dqt = dot_nn(s_far, fk_ref[...])
    dqt_low = dqt.astype(BF)
    neg_dx = (dot_nt(s_near, c) + dot_nt(dqt_low, wb)).astype(BF)
    e = jnp.where(row >= col, -dot_nt(neg_dx, t), 0.0).astype(BF)
    dc = jnp.where(row > col, -dot_tn(x, s_near), 0.0).astype(BF)
    da = jnp.where(row > col, -dot_tn(x, e), 0.0).astype(BF)
    dq = dot_nn(
        jnp.concatenate([s_near, s_far, e], axis=1),
        jnp.concatenate([k, fk_ref[...], w], axis=0),
    )
    dq_ref[...] = dq.astype(BF)
    dk_ref[...] = dot_tn(s_near, q) + dot_tn(dc, wb)
    dwb_ref[...] = dot_nn(dc, k) - dot_tn(x, dqt_low) + dot_nn(da, w)
    dw_ref[...] = dot_tn(e, q) + dot_tn(da, wb)

    @pl.when(pl.program_id(0) == pl.num_programs(0) - 1)
    def finish():
        for copy in moves():
            copy.wait()
        total = mid_ref[...] + own[...].astype(F32)
        for i in range(n - 1):
            total = total + recv[i].astype(F32)
        res_ref[...] = total.astype(BF)


def keys_back_kernel(
    d_ref, bv_ref, q_ref, k_ref, w_ref, b_ref, t_ref, c_ref, h_ref, pre_ref, tap_ref, mark_ref,
    dki_ref, dvi_ref, dwi_ref, dwbi_ref,
    out_ref, tail_ref, dpre_ref, dtap_ref,
):
    length, inner = k_ref.shape
    heads = inner // 128
    row, col = iotas(length, length)
    strict = row > col
    marks = mark_ref[...]
    lanes = lax.broadcasted_iota(jnp.int32, (length, 128), 1)
    side = jnp.zeros((length, 128), F32)
    out_ref[:, :inner] = q_ref[...]
    out_ref[:, 2 * inner : 3 * inner] = (dvi_ref[...] + bv_ref[...].astype(F32)).astype(BF)
    for h in range(heads):
        cols = slice(h * 128, (h + 1) * 128)
        k, w, d, b = k_ref[:, cols], w_ref[:, cols], d_ref[:, cols], b_ref[:, cols]
        wb = (w.astype(F32) * b).astype(BF)
        t, c = t_ref[h], c_ref[h]
        z = dot_tn(t, w).astype(BF)
        dc = jnp.where(strict, -dot_nt(z, d), 0.0).astype(BF)
        f = -dot_nn(t, dot_nn(c, d).astype(BF))
        da = jnp.where(strict, -dot_nt(z, f.astype(BF)), 0.0).astype(BF)
        dk = (dki_ref[:, cols] + d.astype(F32) + dot_tn(dc, wb)).astype(BF)
        out_ref[:, inner + h * 128 : inner + (h + 1) * 128] = dk
        dwb = dwbi_ref[:, cols] + dot_nn(dc, k) + dot_nn(da, w)
        dw = dwi_ref[:, cols] + f + dot_tn(da, wb) + b * dwb
        db = jnp.sum(dwb * w.astype(F32), axis=1, keepdims=True)
        side = jnp.where(lanes == h, db * (b * (1.0 - 0.5 * b)), side)
        taps = tap_ref[:, cols]
        total, shifts = conv_taps(
            h_ref[:, cols].astype(F32), pre_ref[:, cols].astype(F32), taps, marks
        )
        sig = jax.nn.sigmoid(total)
        act = total * sig
        r = lax.rsqrt(jnp.sum(act * act, axis=1, keepdims=True) + 1e-06)
        d_act = r * dw - act * (r * r * r * jnp.sum(act * dw, axis=1, keepdims=True))
        d_total = d_act * sig * (1.0 + total * (1.0 - sig))
        rows = [jnp.sum(d_total * s, axis=0, keepdims=True) for s in shifts]
        dtap_ref[:, cols] = jnp.concatenate(
            rows + [jnp.zeros((8 - len(rows), 128), F32)], axis=0
        )
        pad = jnp.zeros((HALO, 128), F32)
        out = jnp.concatenate([pad, d_total * taps[0:1, :]], axis=0)
        for lag in range(1, taps.shape[0]):
            part = jnp.where(marks[:, lag : lag + 1] > 0.0, d_total, 0.0) * taps[lag : lag + 1, :]
            out = out + pltpu.roll(jnp.concatenate([pad, part], axis=0), length + HALO - lag, 0)
        dpre_ref[:, cols] = out[:HALO, :].astype(BF)
        tail_ref[:, cols] = out[length:, :]
        out_ref[:, 3 * inner + h * 128 : 3 * inner + (h + 1) * 128] = out[HALO:, :].astype(BF)
    out_ref[:, 4 * inner :] = side.astype(BF)


def sds(shape, dtype):
    return jax.ShapeDtypeStruct(shape, dtype)


def cost(micros):
    return pl.CostEstimate(flops=micros * 10**9, bytes_accessed=micros * 10**6, transcendentals=0)


def params():
    return pltpu.CompilerParams(vmem_limit_bytes=56 * 1024 * 1024)


def call_prep(k, hin, prefix, taps, marks, beta):
    length, width = k.shape
    heads = width // 128
    whole = pl.BlockSpec(memory_space=pltpu.VMEM)
    return pl.pallas_call(
        prep_kernel,
        out_shape=(
            sds((length, width), BF),
            sds((heads, length, length), BF),
            sds((heads, length, length), BF),
            sds((length, width), BF),
        ),
        in_specs=[whole] * 6,
        out_specs=[whole] * 4,
        compiler_params=params(),
        cost_estimate=cost(9),
        name="prep",
    )(k, hin, prefix, taps, marks, beta)


def head_specs(length):
    slab = pl.BlockSpec((length, 128), lambda h: (0, h))
    square = pl.BlockSpec((1, length, length), lambda h: (h, 0, 0))
    double = pl.BlockSpec((1, length, 2 * length), lambda h: (h, 0, 0))
    return slab, square, double


def fixed(shape):
    return pl.BlockSpec(shape, lambda h: (0,) * len(shape))


def call_attend(q, k, v, w, beta, t, c, fk, fv, tag_col, tag_rows):
    length, width = q.shape
    heads = width // 128
    slab, square, double = head_specs(length)
    return pl.pallas_call(
        attend_kernel,
        grid=(heads,),
        out_shape=(
            sds((length, width), BF),
            sds((heads, length, 2 * length), BF),
            sds((heads, length, length), BF),
            sds((length, width), BF),
        ),
        in_specs=[slab] * 5
        + [square, square, slab, slab, fixed(tag_col.shape), fixed(tag_rows.shape)],
        out_specs=[slab, double, square, slab],
        compiler_params=params(),
        cost_estimate=cost(11),
        name="attend",
    )(q, k, v, w, beta, t, c, fk, fv, tag_col, tag_rows)


def call_attend_back(n, part, mid, ga, ow, q, k, v, w, beta, t, c, fk, fv, p, x, qt):
    length, width = q.shape
    heads = width // 128
    slab, square, double = head_specs(length)
    flat = (length, width)
    chunk, model = mid.shape
    return pl.pallas_call(
        functools.partial(attend_back_kernel, n),
        grid=(heads,),
        out_shape=(
            sds(flat, BF), sds(flat, F32), sds(flat, F32), sds(flat, F32), sds(flat, F32),
            sds(flat, BF), sds(flat, BF), sds((chunk, model), BF),
        ),
        in_specs=[pl.BlockSpec(memory_space=pl.ANY), fixed(mid.shape), fixed(ga.shape)]
        + [pl.BlockSpec((ow.shape[0], 128), lambda h: (0, h))]
        + [slab] * 5
        + [square, square, slab, slab, double, square, slab],
        out_specs=[slab] * 7 + [fixed((chunk, model))],
        scratch_shapes=[
            pltpu.VMEM((chunk, model), BF),
            pltpu.VMEM((n - 1, chunk, model), BF),
            pltpu.SemaphoreType.DMA,
            pltpu.SemaphoreType.DMA((n - 1,)),
            pltpu.SemaphoreType.DMA((n - 1,)),
        ],
        compiler_params=pltpu.CompilerParams(
            vmem_limit_bytes=56 * 1024 * 1024, collective_id=4, has_side_effects=True
        ),
        cost_estimate=cost(16),
        name="attend_back",
    )(part, mid, ga, ow, q, k, v, w, beta, t, c, fk, fv, p, x, qt)


def call_keys_back(d, back_v, dq, k, w, beta, t, c, hin, prefix, taps, marks, dk, dv, dw, dwb):
    length, width = k.shape
    whole = pl.BlockSpec(memory_space=pltpu.VMEM)
    return pl.pallas_call(
        keys_back_kernel,
        out_shape=(
            sds((length, 4 * width + 128), BF), sds((HALO, width), F32), sds((HALO, width), BF),
            sds((8, width), F32),
        ),
        in_specs=[whole] * 16,
        out_specs=[whole] * 4,
        compiler_params=params(),
        cost_estimate=cost(10),
        name="keys_back",
    )(d, back_v, dq, k, w, beta, t, c, hin, prefix, taps, marks, dk, dv, dw, dwb)


def exchange(n, name, ident, product, operands, specs, extras, finish, rows_out, wide_type, ride):
    length, model = operands[0].shape[0], operands[1].shape[0]
    chunk = length // n
    given = len(operands)
    many = len(extras)
    share = ride is not None
    riders = ride[:2] if share else ()
    width = ride[2] if share else 0

    def body(*refs):
        operand_refs = refs[:given]
        extra_refs = refs[given : given + many]
        start = given + many + len(riders)
        rider_refs = refs[given + many : start]
        last = start + 1 + len(rows_out)
        out_ref, *row_refs = refs[start:last]
        if share:
            ride_outs = refs[last : last + 4]
            last = last + 4
        send, recv, held, send_a, recv_a, send_b, recv_b, *small = refs[last:]
        me = lax.axis_index("tensor")
        barrier = pltpu.get_barrier_semaphore()
        peers = [lax.rem(me + i, n) for i in range(1, n)]
        for peer in peers:
            pl.semaphore_signal(
                barrier, inc=1, device_id={"tensor": peer}, device_id_type=pl.DeviceIdType.MESH
            )
        if share:
            core = lax.axis_index("context")
            other = {"context": 1 - core}
            pl.semaphore_signal(
                barrier, inc=1, device_id=other, device_id_type=pl.DeviceIdType.MESH
            )
        pl.semaphore_wait(barrier, n if share else n - 1)

        def rows_of(index):
            return pl.ds(pl.multiple_of(index * chunk, chunk), chunk)

        if share:
            mine_small, slots, result, held_half, send_c, recv_c, send_d, recv_d, core_sems = small
            row_in, half_in = rider_refs
            rows_half = half_in.shape[0]
            own_half_rows = pl.ds(pl.multiple_of(core * rows_half, rows_half), rows_half)
            swap = pltpu.make_async_remote_copy(
                src_ref=half_in, dst_ref=held_half.at[own_half_rows, :],
                send_sem=core_sems.at[0], recv_sem=core_sems.at[1],
                device_id=other, device_id_type=pl.DeviceIdType.MESH,
            )
            swap.start()

        def partial(index):
            return product(rows_of(index), *operand_refs)

        first = []
        for i, peer in enumerate(peers):
            send[i] = partial(peer).astype(BF)
            copy = pltpu.make_async_remote_copy(
                src_ref=send.at[i], dst_ref=recv.at[i],
                send_sem=send_a.at[i], recv_sem=recv_a.at[i],
                device_id={"tensor": peer}, device_id_type=pl.DeviceIdType.MESH,
            )
            copy.start()
            first.append(copy)
        total = partial(me)
        for i, copy in enumerate(first):
            copy.wait()
            total = total + recv[i].astype(F32)
        mine = rows_of(me)
        done, *row_values = finish(total, mine, *extra_refs)
        held[mine, :] = done.astype(BF)
        second = []
        for i, peer in enumerate(peers):
            copy = pltpu.make_async_remote_copy(
                src_ref=held.at[mine, :], dst_ref=held.at[mine, :],
                send_sem=send_b.at[i], recv_sem=recv_b.at[i],
                device_id={"tensor": peer}, device_id_type=pl.DeviceIdType.MESH,
            )
            copy.start()
            second.append(copy)
        if share:
            fourth = []
            for i, peer in enumerate(peers):
                copy = pltpu.make_async_remote_copy(
                    src_ref=row_in, dst_ref=result.at[mine, :],
                    send_sem=send_d.at[i], recv_sem=recv_d.at[i],
                    device_id={"tensor": peer}, device_id_type=pl.DeviceIdType.MESH,
                )
                copy.start()
                fourth.append(copy)
            mine_small[...] = row_values[-1]
            slots[me] = row_values[-1]
            third = []
            for i, peer in enumerate(peers):
                copy = pltpu.make_async_remote_copy(
                    src_ref=mine_small, dst_ref=slots.at[me],
                    send_sem=send_c.at[i], recv_sem=recv_c.at[i],
                    device_id={"tensor": peer}, device_id_type=pl.DeviceIdType.MESH,
                )
                copy.start()
                third.append(copy)
        for ref, value in zip(row_refs, row_values):
            ref[...] = value
        if share:
            result[mine, :] = row_in[...]
            held_half[own_half_rows, :] = half_in[...]
            swap.wait()
            res_ref, gate_ref, up_ref, down_ref = ride_outs
            for j in range(gate_ref.shape[1] // width):
                at, to = 3 * width * j, slice(j * width, (j + 1) * width)
                gate_ref[:, to] = held_half[:, at : at + width].astype(F32)
                up_ref[:, to] = held_half[:, at + width : at + 2 * width].astype(F32)
                turned = held_half[:, at + 2 * width : at + 3 * width].astype(F32).T
                down_ref[to, :] = turned
            for copy in third:
                copy.wait()
            row_refs[-1][...] = sum(slots[i] for i in range(n))
        for copy in second:
            copy.wait()
        out_ref[...] = held[...].astype(wide_type)
        if share:
            for copy in fourth:
                copy.wait()
            res_ref[...] = result[...]

    ride_shapes = ()
    if share:
        deep_rows, hidden = 2 * ride[1].shape[0], ride[1].shape[1] // 3
        ride_shapes = (
            sds((length, model), BF), sds((deep_rows, hidden), F32), sds((deep_rows, hidden), F32),
            sds((hidden, deep_rows), F32),
        )
    whole = pl.BlockSpec(memory_space=pltpu.VMEM)
    return pl.pallas_call(
        body,
        out_shape=(sds((length, model), wide_type),)
        + tuple(sds((chunk if r is None else r, model), F32) for r in rows_out)
        + ride_shapes,
        in_specs=[whole if spec is None else spec for spec in specs] + [whole] * (many + len(riders)),
        out_specs=[whole] * (1 + len(rows_out) + len(ride_shapes)),
        scratch_shapes=[
            pltpu.VMEM((n - 1, chunk, model), BF),
            pltpu.VMEM((n - 1, chunk, model), BF),
            pltpu.VMEM((length, model), BF),
            pltpu.SemaphoreType.DMA((n - 1,)),
            pltpu.SemaphoreType.DMA((n - 1,)),
            pltpu.SemaphoreType.DMA((n - 1,)),
            pltpu.SemaphoreType.DMA((n - 1,)),
        ]
        + (
            [
                pltpu.VMEM((8, model), F32),
                pltpu.VMEM((n, 8, model), F32),
                pltpu.VMEM((length, model), BF),
                pltpu.VMEM((2 * ride[1].shape[0], ride[1].shape[1]), BF),
                pltpu.SemaphoreType.DMA((n - 1,)),
                pltpu.SemaphoreType.DMA((n - 1,)),
                pltpu.SemaphoreType.DMA((n - 1,)),
                pltpu.SemaphoreType.DMA((n - 1,)),
                pltpu.SemaphoreType.DMA((2,)),
            ]
            if share
            else []
        ),
        compiler_params=pltpu.CompilerParams(
            vmem_limit_bytes=56 * 1024 * 1024, collective_id=ident, has_side_effects=True
        ),
        cost_estimate=cost(40),
        name=name,
    )(*operands, *extras, *riders)


def inverse_rms(x):
    return lax.rsqrt(jnp.mean(x * x, axis=1, keepdims=True) + 1e-06)


def finish_middle(total, mine, tokens_ref, gain_ref):
    middle = tokens_ref[mine, :].astype(F32) + total
    return middle * inverse_rms(middle) * gain_ref[0:1, :], middle


def norm_back(grad, x, gain):
    r = inverse_rms(x)
    g = grad * gain
    out = r * g - x * (r * r * r * jnp.mean(g * x, axis=1, keepdims=True))
    gain_grad = jnp.sum(grad * x * r, axis=0, keepdims=True)
    return out, jnp.broadcast_to(gain_grad, (8, gain_grad.shape[1]))


def finish_second(total, mine, middle_ref, cot_ref, gain_ref):
    out, gain_grad = norm_back(total, middle_ref[...], gain_ref[0:1, :])
    grad = cot_ref[mine, :].astype(F32) + out
    return grad, grad, gain_grad


def finish_first(total, mine, tokens_ref, grad_ref, gain_ref, second_ref):
    out, gain_grad = norm_back(total, tokens_ref[mine, :].astype(F32), gain_ref[0:1, :])
    row = lax.broadcasted_iota(jnp.int32, gain_grad.shape, 0)
    return grad_ref[...] + out, jnp.where(row == 0, gain_grad, second_ref[...])


def tail_nt(first):
    def product(rows, lhs_ref, rhs_ref):
        width = lhs_ref.shape[1]
        return dot_nt(lhs_ref[rows, :], rhs_ref[:, first : first + width])

    return product


def blocks_nt(width, offset, stride):
    def product(rows, lhs_ref, rhs_ref):
        total = None
        for j in range(lhs_ref.shape[1] // width):
            at = j * stride + offset
            term = dot_nt(lhs_ref[rows, j * width : (j + 1) * width], rhs_ref[:, at : at + width])
            total = term if total is None else total + term
        return total

    return product


def last_kernel(
    deep, cores, x_ref, half_ref, gain_ref, out_ref, q_ref, k_ref, v_ref, h_ref, side_ref,
    slots, held, send_sem, recv_sem, core_sems,
):
    z, core = lax.axis_index("fsdp"), lax.axis_index("context")
    me = z * cores + core
    count = deep * cores
    barrier = pltpu.get_barrier_semaphore()
    peers = []
    for i in range(1, count):
        peer = lax.rem(me + i, count)
        peers.append({"fsdp": peer // cores, "context": lax.rem(peer, cores)})
    for peer in peers:
        pl.semaphore_signal(barrier, inc=1, device_id=peer, device_id_type=pl.DeviceIdType.MESH)
    pl.semaphore_wait(barrier, count - 1)
    rows_half = half_ref.shape[0]
    own = pl.ds(pl.multiple_of(core * rows_half, rows_half), rows_half)
    swap = pltpu.make_async_remote_copy(
        src_ref=half_ref, dst_ref=held.at[own, :],
        send_sem=core_sems.at[0], recv_sem=core_sems.at[1],
        device_id={"context": 1 - core}, device_id_type=pl.DeviceIdType.MESH,
    )
    swap.start()
    copies = []
    for i, peer in enumerate(peers):
        copy = pltpu.make_async_remote_copy(
            src_ref=x_ref.at[peer["fsdp"]], dst_ref=slots.at[me],
            send_sem=send_sem.at[i], recv_sem=recv_sem.at[i],
            device_id=peer, device_id_type=pl.DeviceIdType.MESH,
        )
        copy.start()
        copies.append(copy)
    slots[me] = x_ref[z]
    held[own, :] = half_ref[...]
    swap.wait()
    inner = q_ref.shape[1]
    out_ref[...] = held[:, :inner].astype(F32).T
    for i, ref in enumerate((q_ref, k_ref, v_ref, h_ref)):
        ref[...] = held[:, (i + 1) * inner : (i + 2) * inner].astype(F32)
    side_ref[...] = held[:, 5 * inner :].astype(F32)
    for copy in copies:
        copy.wait()
    gain_ref[...] = sum(slots[i] for i in range(count))


def call_last(x, half, inner, cores):
    deep, eight, rows = x.shape
    count = deep * cores
    full = cores * half.shape[0]
    whole = pl.BlockSpec(memory_space=pltpu.VMEM)
    return pl.pallas_call(
        functools.partial(last_kernel, deep, cores),
        out_shape=(sds((eight, rows), F32), sds((inner, full), F32))
        + (sds((full, inner), F32),) * 4
        + (sds((full, half.shape[1] - 5 * inner), F32),),
        in_specs=[whole] * 2,
        out_specs=[whole] * 7,
        scratch_shapes=[
            pltpu.VMEM((count, eight, rows), F32),
            pltpu.VMEM((full, half.shape[1]), BF),
            pltpu.SemaphoreType.DMA((count - 1,)),
            pltpu.SemaphoreType.DMA((count - 1,)),
            pltpu.SemaphoreType.DMA((2,)),
        ],
        compiler_params=pltpu.CompilerParams(collective_id=5, has_side_effects=True),
        cost_estimate=cost(8),
        name="last",
    )(x, half)


def ffn_kernel(n_ref, cot_ref, w_ref, part_ref, gb_ref, gw_ref, nt, ct, acc):
    width = w_ref.shape[1] // 3

    @pl.when(pl.program_id(0) == 0)
    def turn():
        nt[...] = n_ref[...].T
        ct[...] = cot_ref[...].T
        acc[...] = jnp.zeros_like(acc)

    both = dot_nn(n_ref[...], w_ref[:, : 2 * width])
    gate, up = both[:, :width], both[:, width:]
    back = dot_nn(cot_ref[...], w_ref[:, 2 * width :])
    sig = jax.nn.sigmoid(gate)
    act = gate * sig
    hidden = (act * up).astype(BF)
    acc[...] += dot_nt(hidden, w_ref[:, 2 * width :])
    grad = jnp.concatenate(
        [(back * up * (sig + act * (1.0 - sig))).astype(BF), (back * act).astype(BF)], axis=1
    )
    gb_ref[...] = grad
    gw_ref[:, : 2 * width] = dot_nn(nt[...], grad).astype(BF)
    gw_ref[:, 2 * width :] = dot_nn(ct[...], hidden).astype(BF)

    @pl.when(pl.program_id(0) == pl.num_programs(0) - 1)
    def close():
        part_ref[...] = acc[...].astype(BF)


def call_ffn(normed, cot, weights, width):
    length, model = normed.shape
    steps = weights.shape[1] // (3 * width)
    return pl.pallas_call(
        ffn_kernel,
        grid=(steps,),
        out_shape=(
            sds((length, model), BF),
            sds((length, steps * 2 * width), BF),
            sds(weights.shape, BF),
        ),
        in_specs=[
            fixed(normed.shape), fixed(cot.shape),
            pl.BlockSpec((model, 3 * width), lambda j: (0, j)),
        ],
        out_specs=[
            fixed((length, model)),
            pl.BlockSpec((length, 2 * width), lambda j: (0, j)),
            pl.BlockSpec((model, 3 * width), lambda j: (0, j)),
        ],
        scratch_shapes=[
            pltpu.VMEM((model, length), BF),
            pltpu.VMEM((model, length), BF),
            pltpu.VMEM((length, model), F32),
        ],
        compiler_params=params(),
        cost_estimate=cost(14),
        name="ffn",
    )(normed, cot, weights)


def grads_kernel(lane, n_ref, ga_ref, d_ref, m_ref, conv_ref, out_ref):
    inner = m_ref.shape[1]
    main = d_ref.shape[1] - 128
    out_ref[:, :inner] = dot_tn(ga_ref[...], m_ref[...]).astype(BF)
    out_ref[:, inner : inner + main] = dot_tn(n_ref[...], d_ref[:, :main]).astype(BF)
    side = dot_tn(n_ref[...], d_ref[:, main:])
    lanes = lax.broadcasted_iota(jnp.int32, side.shape, 1)
    out_ref[:, inner + main :] = jnp.where(lanes == lane, conv_ref[...], side).astype(BF)


def call_grads(lane, normed, ga, dproj, mixed, dconv):
    length, model = normed.shape
    block = 384
    wide = dproj.shape[1] + mixed.shape[1]
    part = pl.BlockSpec((length, block), lambda i: (0, i))
    return pl.pallas_call(
        functools.partial(grads_kernel, lane),
        grid=(model // block,),
        out_shape=sds((model, wide), BF),
        in_specs=[
            part, part, fixed(dproj.shape), fixed(mixed.shape),
            pl.BlockSpec((block, 1), lambda i: (i, 0)),
        ],
        out_specs=pl.BlockSpec((block, wide), lambda i: (i, 0)),
        compiler_params=params(),
        cost_estimate=cost(7),
        name="grads",
    )(normed, ga, dproj, mixed, dconv)


def shift_to(value, axis, steps):
    count = lax.axis_size(axis)
    leading, last = (max(0, -steps), min(count, count - steps))
    return lax.ppermute(value, axis, [(at, at + steps) for at in range(leading, last)])


def own_half(value):
    rows = value.shape[0] // lax.axis_size("context")
    return lax.dynamic_slice_in_dim(value, lax.axis_index("context") * rows, rows, axis=0)


def gather_rows(value):
    return lax.all_gather(own_half(value), ("fsdp", "context"), axis=0, tiled=True)


def scatter_half(value):
    return lax.psum_scatter(value, ("fsdp", "context"), scatter_dimension=0, tiled=True)


FBLOCK = 256


def on_device(
    tokens,
    segments,
    cotangent,
    query_weight,
    key_weight,
    value_weight,
    house_weight,
    beta_weight,
    conv_weight,
    output_weight,
    gate_weight,
    up_weight,
    down_weight,
    first_gain,
    second_gain,
):
    seq_count, length, model = tokens.shape
    rows = first_gain.shape[0]
    deep = lax.axis_size("fsdp")
    inner = query_weight.shape[1]
    heads, tap_count, chans = conv_weight.shape
    assert seq_count == 1 and heads * tap_count * chans == rows
    side = jnp.concatenate(
        [
            beta_weight,
            first_gain[:, None],
            second_gain[:, None],
            conv_weight.reshape(rows, 1),
            jnp.zeros((rows, 128 - heads - 3), BF),
        ],
        axis=1,
    )
    pack = gather_rows(
        jnp.concatenate(
            [output_weight.T, query_weight, key_weight, value_weight, house_weight, side], axis=1
        )
    )
    hidden_width = gate_weight.shape[1]
    steps = hidden_width // FBLOCK
    down_t = down_weight.T
    ffn_w = gather_rows(
        jnp.concatenate(
            [
                part[:, j * FBLOCK : (j + 1) * FBLOCK]
                for j in range(steps)
                for part in (gate_weight, up_weight, down_t)
            ],
            axis=1,
        )
    )
    side_full = pack[:, 5 * inner :]
    gain_one = side_full[:, heads].astype(F32)
    gain_two = side_full[:, heads + 1].astype(F32)
    taps = jnp.transpose(
        side_full[:, heads + 2].reshape(deep, heads, tap_count, chans), (2, 1, 0, 3)
    ).reshape(tap_count, inner).astype(F32)

    tags = (segments[0] + 1).astype(F32)
    far_tags = shift_to(tags, "context", 1)
    near_tags = jnp.concatenate([far_tags[length - tap_count + 1 :], tags])
    marks = jnp.stack(
        [
            near_tags[tap_count - 1 - lag : tap_count - 1 - lag + length] == tags
            for lag in range(tap_count)
        ],
        axis=1,
    ).astype(F32)

    stream = tokens[0].astype(F32)
    scale_one = lax.rsqrt(jnp.mean(stream * stream, axis=1, keepdims=True) + 1e-06)
    normed = (stream * scale_one * gain_one).astype(BF)
    proj = dot_nn(normed, pack[:, inner : 5 * inner]).astype(BF)
    beta_raw = dot_nn(normed, side_full)[:, :heads]
    beta = jnp.repeat(2.0 * jax.nn.sigmoid(beta_raw), 128, axis=1)
    q, k, v, hin = (proj[:, i * inner : (i + 1) * inner] for i in range(4))
    prefix = shift_to(hin[length - HALO :], "context", 1)
    w, t, c, sent = call_prep(k, hin, prefix, taps, marks, beta)
    far_k = shift_to(sent, "context", 1)
    far_v = shift_to(v, "context", 1)
    mixed, probs, x, qt = call_attend(
        q, k, v, w, beta, t, c, far_k, far_v, tags[:, None], jnp.stack([tags, far_tags])
    )
    n = lax.axis_size("tensor")
    rows_one = jnp.broadcast_to(gain_one[None, :], (8, model))
    rows_two = jnp.broadcast_to(gain_two[None, :], (8, model))
    normed_two, middle = exchange(
        n, "sum_mixed", 1, tail_nt(0), (mixed, pack),
        (None, None), (tokens[0], rows_two),
        finish_middle, (None,), BF, None,
    )
    cot = cotangent[0]
    part, grad_both, grad_ffn = call_ffn(normed_two, cot, ffn_w, FBLOCK)
    grad_both, grad_ffn = lax.optimization_barrier((grad_both, grad_ffn))
    grad_ffn = scatter_half(grad_ffn)
    grad_attn, grad_middle, grad_second = exchange(
        n, "sum_second", 2, blocks_nt(2 * FBLOCK, 0, 3 * FBLOCK), (grad_both, ffn_w),
        (None, None), (middle, cot, rows_two), finish_second, (None, 8), BF, None,
    )

    dq, dk, dv, dw, dwb, dfk, dfv, finished = call_attend_back(
        n, part, middle, grad_attn, pack, q, k, v, w, beta, t, c, far_k, far_v, probs, x, qt
    )
    back_k = shift_to(dfk, "context", -1)
    back_v = shift_to(dfv, "context", -1)
    dproj, tail, dpre, dtap = call_keys_back(
        back_k, back_v, dq, k, w, beta, t, c, hin, prefix, taps, marks, dk, dv, dw, dwb
    )
    back_pre = shift_to(dpre, "context", -1).astype(F32)
    dproj = lax.dynamic_update_slice(
        dproj, (tail + back_pre).astype(BF), (length - HALO, 3 * inner)
    )
    dconv = jnp.transpose(
        dtap[:tap_count].reshape(tap_count, heads, deep, chans), (2, 1, 0, 3)
    ).reshape(model, 1)
    grad_pack = call_grads(heads + 2, normed, grad_attn, dproj, mixed, dconv)
    dproj, grad_pack, grad_ffn = lax.optimization_barrier((dproj, grad_pack, grad_ffn))
    grad_pack = scatter_half(grad_pack)
    grad_input, gains, result, gate_grad, up_grad, down_grad = exchange(
        n, "sum_first", 3, tail_nt(inner), (dproj, pack), (None, None),
        (tokens[0], grad_middle, rows_one, grad_second), finish_first, (8,), F32,
        (finished, grad_ffn, FBLOCK),
    )
    gains = jnp.transpose(gains.reshape(8, deep, rows), (1, 0, 2))
    gains, out_grad, q_grad, k_grad, v_grad, h_grad, side_grad = call_last(
        gains, grad_pack, inner, lax.axis_size("context")
    )
    return (
        result.reshape(tokens.shape),
        grad_input.reshape(tokens.shape),
        q_grad,
        k_grad,
        v_grad,
        h_grad,
        side_grad[:, :heads],
        side_grad[:, heads + 2].reshape(conv_weight.shape),
        out_grad,
        gate_grad,
        up_grad,
        down_grad,
        gains[0],
        gains[1],
    )


def solution(mesh):
    in_specs = (
        P("fsdp", "context", None),
        P("fsdp", "context"),
        P("fsdp", "context", None),
        P("fsdp", "tensor"),
        P("fsdp", "tensor"),
        P("fsdp", "tensor"),
        P("fsdp", "tensor"),
        P("fsdp", "tensor"),
        P("tensor", None, "fsdp"),
        P("tensor", "fsdp"),
        P("fsdp", "tensor"),
        P("fsdp", "tensor"),
        P("tensor", "fsdp"),
        P("fsdp"),
        P("fsdp"),
    )
    out_specs = (
        P("fsdp", "context", None),
        P("fsdp", "context", None),
        P("fsdp", "tensor"),
        P("fsdp", "tensor"),
        P("fsdp", "tensor"),
        P("fsdp", "tensor"),
        P("fsdp", "tensor"),
        P("tensor", None, "fsdp"),
        P("tensor", "fsdp"),
        P("fsdp", "tensor"),
        P("fsdp", "tensor"),
        P("tensor", "fsdp"),
        P("fsdp"),
        P("fsdp"),
    )
    return jax.shard_map(
        on_device, mesh=mesh, in_specs=in_specs, out_specs=out_specs, check_vma=False
    )
```

```python
import functools
import math

import jax
import jax.numpy as jnp
from jax import lax
from jax.experimental import pallas as pl
from jax.experimental.pallas import tpu as pltpu
from jax.sharding import PartitionSpec as P

BF = jnp.bfloat16
F32 = jnp.float32
HALO = 16


def dot_nn(a, b):
    return jnp.dot(a, b, preferred_element_type=F32)


def dot_nt(a, b):
    return lax.dot_general(a, b, (((1,), (1,)), ((), ())), preferred_element_type=F32)


def dot_tn(a, b):
    return lax.dot_general(a, b, (((0,), (0,)), ((), ())), preferred_element_type=F32)


def iotas(rows, cols):
    return (
        lax.broadcasted_iota(jnp.int32, (rows, cols), 0),
        lax.broadcasted_iota(jnp.int32, (rows, cols), 1),
    )


def unit_lower_inverse(blocks, size):
    row, col = iotas(size, size)
    diff = row ^ col
    eye = jnp.where(row == col, 1.0, 0.0).astype(F32)
    low = row > col
    inv = [eye - jnp.where(low & (diff < 2), a, 0.0) for a in blocks]
    span = 2
    while span < size:
        pick = low & (diff >= span) & (diff < 2 * span)
        off = [jnp.where(pick, a, 0.0).astype(BF) for a in blocks]
        held = [t.astype(BF) for t in inv]
        step = [dot_nn(h, o).astype(BF) for h, o in zip(held, off)]
        inv = [t - dot_nn(s, h) for t, s, h in zip(inv, step, held)]
        span *= 2
    return inv


def conv_taps(hin, prefix, taps, marks):
    ext = jnp.concatenate([prefix, hin], axis=0)
    shifts = [hin]
    total = hin * taps[0:1, :]
    for lag in range(1, taps.shape[0]):
        moved = pltpu.roll(ext, lag, 0)[HALO:, :]
        moved = jnp.where(marks[:, lag : lag + 1] > 0.0, moved, 0.0)
        shifts.append(moved)
        total = total + moved * taps[lag : lag + 1, :]
    return total, shifts


def prep_kernel(k_ref, h_ref, pre_ref, tap_ref, mark_ref, b_ref, w_ref, t_ref, c_ref, sent_ref):
    length = k_ref.shape[0]
    half = length // 2
    quarter = length // 4
    heads = t_ref.shape[0]
    row, col = iotas(length, length)
    strict = row > col
    total, unused = conv_taps(
        h_ref[...].astype(F32), pre_ref[...].astype(F32), tap_ref[...], mark_ref[...]
    )
    act = total * jax.nn.sigmoid(total)
    houses, blocks, coupled = [], [], []
    for h in range(heads):
        cols = slice(h * 128, (h + 1) * 128)
        a = act[:, cols]
        w = (a * lax.rsqrt(jnp.sum(a * a, axis=1, keepdims=True) + 1e-06)).astype(BF)
        w_ref[:, cols] = w
        houses.append(w)
        full = jnp.where(strict, dot_nt(w, w) * b_ref[:, h * 128 : h * 128 + 1], 0.0)
        coupled.append(full.astype(BF))
        for q in range(4):
            blocks.append(full[q * quarter : (q + 1) * quarter, q * quarter : (q + 1) * quarter])
    inv = unit_lower_inverse(blocks, quarter)
    for h in range(heads):
        cols = slice(h * 128, (h + 1) * 128)
        diag = [t.astype(BF) for t in inv[4 * h : 4 * h + 4]]
        halves = []
        for p in range(2):
            at = p * half
            off = coupled[h][at + quarter : at + half, at : at + quarter]
            corner = -dot_nn(dot_nn(diag[2 * p + 1], off).astype(BF), diag[2 * p])
            zero = jnp.zeros((quarter, quarter), BF)
            halves.append(
                jnp.concatenate(
                    [
                        jnp.concatenate([diag[2 * p], zero], axis=1),
                        jnp.concatenate([corner.astype(BF), diag[2 * p + 1]], axis=1),
                    ],
                    axis=0,
                )
            )
        off = coupled[h][half:, :half]
        corner = -dot_nn(dot_nn(halves[1], off).astype(BF), halves[0])
        t_full = jnp.concatenate(
            [
                jnp.concatenate([halves[0], jnp.zeros((half, half), BF)], axis=1),
                jnp.concatenate([corner.astype(BF), halves[1]], axis=1),
            ],
            axis=0,
        )
        t_ref[h] = t_full
        w = houses[h]
        k = k_ref[:, cols]
        c = jnp.where(strict, dot_nt(w, k) * b_ref[:, h * 128 : h * 128 + 1], 0.0).astype(BF)
        c_ref[h] = c
        z = dot_tn(t_full, w).astype(BF)
        sent_ref[:, cols] = (k.astype(F32) - dot_tn(c, z)).astype(BF)


def attend_kernel(
    q_ref, k_ref, v_ref, w_ref, b_ref, t_ref, c_ref, fk_ref, fv_ref, tc_ref, tr_ref,
    o_ref, p_ref, x_ref, qt_ref,
):
    length = q_ref.shape[0]
    row, col = iotas(length, length)
    causal = row >= col
    q, k, w = q_ref[...], k_ref[...], w_ref[...]
    wb = (w.astype(F32) * b_ref[...]).astype(BF)
    reach = jnp.where(causal, dot_nt(q, w), 0.0).astype(BF)
    x = dot_nn(reach, t_ref[0]).astype(BF)
    x_ref[0] = x
    qt = (q.astype(F32) - dot_nn(x, wb)).astype(BF)
    qt_ref[...] = qt
    scale = 1.0 / math.sqrt(q.shape[1])
    tags = tc_ref[...]
    near = jnp.where(
        causal & (tags == tr_ref[0:1, :]), (dot_nt(q, k) - dot_nn(x, c_ref[0])) * scale, -1e30
    )
    far = jnp.where(tags == tr_ref[1:2, :], dot_nt(qt, fk_ref[...]) * scale, -1e30)
    top = jnp.maximum(
        jnp.max(near, axis=1, keepdims=True), jnp.max(far, axis=1, keepdims=True)
    )
    near = jnp.exp(near - top)
    far = jnp.exp(far - top)
    inv = 1.0 / (jnp.sum(near, axis=1, keepdims=True) + jnp.sum(far, axis=1, keepdims=True))
    near = (near * inv).astype(BF)
    far = (far * inv).astype(BF)
    p_ref[0, :, :length] = near
    p_ref[0, :, length:] = far
    o_ref[...] = (dot_nn(near, v_ref[...]) + dot_nn(far, fv_ref[...])).astype(BF)


def attend_back_kernel(
    n, part_ref, mid_ref, ga_ref, ow_ref, q_ref, k_ref, v_ref, w_ref, b_ref, t_ref, c_ref, fk_ref, fv_ref, p_ref, x_ref,
    qt_ref,
    dq_ref, dk_ref, dv_ref, dw_ref, dwb_ref, dfk_ref, dfv_ref, res_ref,
    own, recv, own_sem, send_sem, recv_sem,
):
    length = q_ref.shape[0]
    chunk = length // n
    me = lax.axis_index("tensor")

    def rows_of(index):
        return pl.ds(pl.multiple_of(index * chunk, chunk), chunk)

    def moves():
        out = [pltpu.make_async_copy(part_ref.at[rows_of(me), :], own, own_sem)]
        for i in range(1, n):
            peer = lax.rem(me + i, n)
            out.append(
                pltpu.make_async_remote_copy(
                    src_ref=part_ref.at[rows_of(peer), :], dst_ref=recv.at[i - 1],
                    send_sem=send_sem.at[i - 1], recv_sem=recv_sem.at[i - 1],
                    device_id={"tensor": peer}, device_id_type=pl.DeviceIdType.MESH,
                )
            )
        return out

    @pl.when(pl.program_id(0) == 0)
    def begin():
        barrier = pltpu.get_barrier_semaphore()
        for i in range(1, n):
            pl.semaphore_signal(
                barrier, inc=1, device_id={"tensor": lax.rem(me + i, n)},
                device_id_type=pl.DeviceIdType.MESH,
            )
        pl.semaphore_wait(barrier, n - 1)
        for copy in moves():
            copy.start()

    row, col = iotas(length, length)
    q, k, w = q_ref[...], k_ref[...], w_ref[...]
    g = dot_nn(ga_ref[...], ow_ref[...]).astype(BF)
    wb = (w.astype(F32) * b_ref[...]).astype(BF)
    x, t, c = x_ref[0], t_ref[0], c_ref[0]
    near, far = p_ref[0, :, :length], p_ref[0, :, length:]
    dv_ref[...] = dot_tn(near, g)
    dfv_ref[...] = dot_tn(far, g).astype(BF)
    d_near = dot_nt(g, v_ref[...])
    d_far = dot_nt(g, fv_ref[...])
    near, far = near.astype(F32), far.astype(F32)
    mean = jnp.sum(near * d_near, axis=1, keepdims=True) + jnp.sum(
        far * d_far, axis=1, keepdims=True
    )
    scale = 1.0 / math.sqrt(q.shape[1])
    s_near = (near * (d_near - mean) * scale).astype(BF)
    s_far = (far * (d_far - mean) * scale).astype(BF)
    dfk_ref[...] = dot_tn(s_far, qt_ref[...]).astype(BF)
    dqt = dot_nn(s_far, fk_ref[...])
    dqt_low = dqt.astype(BF)
    neg_dx = (dot_nt(s_near, c) + dot_nt(dqt_low, wb)).astype(BF)
    e = jnp.where(row >= col, -dot_nt(neg_dx, t), 0.0).astype(BF)
    dc = jnp.where(row > col, -dot_tn(x, s_near), 0.0).astype(BF)
    da = jnp.where(row > col, -dot_tn(x, e), 0.0).astype(BF)
    dq = dot_nn(
        jnp.concatenate([s_near, s_far, e], axis=1),
        jnp.concatenate([k, fk_ref[...], w], axis=0),
    )
    dq_ref[...] = dq.astype(BF)
    dk_ref[...] = dot_tn(s_near, q) + dot_tn(dc, wb)
    dwb_ref[...] = dot_nn(dc, k) - dot_tn(x, dqt_low) + dot_nn(da, w)
    dw_ref[...] = dot_tn(e, q) + dot_tn(da, wb)

    @pl.when(pl.program_id(0) == pl.num_programs(0) - 1)
    def finish():
        for copy in moves():
            copy.wait()
        total = mid_ref[...] + own[...].astype(F32)
        for i in range(n - 1):
            total = total + recv[i].astype(F32)
        res_ref[...] = total.astype(BF)


def keys_back_kernel(
    d_ref, bv_ref, q_ref, k_ref, w_ref, b_ref, t_ref, c_ref, h_ref, pre_ref, tap_ref, mark_ref,
    dki_ref, dvi_ref, dwi_ref, dwbi_ref,
    out_ref, tail_ref, dpre_ref, dtap_ref,
):
    length, inner = k_ref.shape
    heads = inner // 128
    row, col = iotas(length, length)
    strict = row > col
    marks = mark_ref[...]
    lanes = lax.broadcasted_iota(jnp.int32, (length, 128), 1)
    side = jnp.zeros((length, 128), F32)
    out_ref[:, :inner] = q_ref[...]
    out_ref[:, 2 * inner : 3 * inner] = (dvi_ref[...] + bv_ref[...].astype(F32)).astype(BF)
    for h in range(heads):
        cols = slice(h * 128, (h + 1) * 128)
        k, w, d, b = k_ref[:, cols], w_ref[:, cols], d_ref[:, cols], b_ref[:, cols]
        wb = (w.astype(F32) * b).astype(BF)
        t, c = t_ref[h], c_ref[h]
        z = dot_tn(t, w).astype(BF)
        dc = jnp.where(strict, -dot_nt(z, d), 0.0).astype(BF)
        f = -dot_nn(t, dot_nn(c, d).astype(BF))
        da = jnp.where(strict, -dot_nt(z, f.astype(BF)), 0.0).astype(BF)
        dk = (dki_ref[:, cols] + d.astype(F32) + dot_tn(dc, wb)).astype(BF)
        out_ref[:, inner + h * 128 : inner + (h + 1) * 128] = dk
        dwb = dwbi_ref[:, cols] + dot_nn(dc, k) + dot_nn(da, w)
        dw = dwi_ref[:, cols] + f + dot_tn(da, wb) + b * dwb
        db = jnp.sum(dwb * w.astype(F32), axis=1, keepdims=True)
        side = jnp.where(lanes == h, db * (b * (1.0 - 0.5 * b)), side)
        taps = tap_ref[:, cols]
        total, shifts = conv_taps(
            h_ref[:, cols].astype(F32), pre_ref[:, cols].astype(F32), taps, marks
        )
        sig = jax.nn.sigmoid(total)
        act = total * sig
        r = lax.rsqrt(jnp.sum(act * act, axis=1, keepdims=True) + 1e-06)
        d_act = r * dw - act * (r * r * r * jnp.sum(act * dw, axis=1, keepdims=True))
        d_total = d_act * sig * (1.0 + total * (1.0 - sig))
        rows = [jnp.sum(d_total * s, axis=0, keepdims=True) for s in shifts]
        dtap_ref[:, cols] = jnp.concatenate(
            rows + [jnp.zeros((8 - len(rows), 128), F32)], axis=0
        )
        pad = jnp.zeros((HALO, 128), F32)
        out = jnp.concatenate([pad, d_total * taps[0:1, :]], axis=0)
        for lag in range(1, taps.shape[0]):
            part = jnp.where(marks[:, lag : lag + 1] > 0.0, d_total, 0.0) * taps[lag : lag + 1, :]
            out = out + pltpu.roll(jnp.concatenate([pad, part], axis=0), length + HALO - lag, 0)
        dpre_ref[:, cols] = out[:HALO, :].astype(BF)
        tail_ref[:, cols] = out[length:, :]
        out_ref[:, 3 * inner + h * 128 : 3 * inner + (h + 1) * 128] = out[HALO:, :].astype(BF)
    out_ref[:, 4 * inner :] = side.astype(BF)


def sds(shape, dtype):
    return jax.ShapeDtypeStruct(shape, dtype)


def cost(micros):
    return pl.CostEstimate(flops=micros * 10**9, bytes_accessed=micros * 10**6, transcendentals=0)


def params():
    return pltpu.CompilerParams(vmem_limit_bytes=56 * 1024 * 1024)


def call_prep(k, hin, prefix, taps, marks, beta):
    length, width = k.shape
    heads = width // 128
    whole = pl.BlockSpec(memory_space=pltpu.VMEM)
    return pl.pallas_call(
        prep_kernel,
        out_shape=(
            sds((length, width), BF),
            sds((heads, length, length), BF),
            sds((heads, length, length), BF),
            sds((length, width), BF),
        ),
        in_specs=[whole] * 6,
        out_specs=[whole] * 4,
        compiler_params=params(),
        cost_estimate=cost(9),
        name="prep",
    )(k, hin, prefix, taps, marks, beta)


def head_specs(length):
    slab = pl.BlockSpec((length, 128), lambda h: (0, h))
    square = pl.BlockSpec((1, length, length), lambda h: (h, 0, 0))
    double = pl.BlockSpec((1, length, 2 * length), lambda h: (h, 0, 0))
    return slab, square, double


def fixed(shape):
    return pl.BlockSpec(shape, lambda h: (0,) * len(shape))


def call_attend(q, k, v, w, beta, t, c, fk, fv, tag_col, tag_rows):
    length, width = q.shape
    heads = width // 128
    slab, square, double = head_specs(length)
    return pl.pallas_call(
        attend_kernel,
        grid=(heads,),
        out_shape=(
            sds((length, width), BF),
            sds((heads, length, 2 * length), BF),
            sds((heads, length, length), BF),
            sds((length, width), BF),
        ),
        in_specs=[slab] * 5
        + [square, square, slab, slab, fixed(tag_col.shape), fixed(tag_rows.shape)],
        out_specs=[slab, double, square, slab],
        compiler_params=params(),
        cost_estimate=cost(11),
        name="attend",
    )(q, k, v, w, beta, t, c, fk, fv, tag_col, tag_rows)


def call_attend_back(n, part, mid, ga, ow, q, k, v, w, beta, t, c, fk, fv, p, x, qt):
    length, width = q.shape
    heads = width // 128
    slab, square, double = head_specs(length)
    flat = (length, width)
    chunk, model = mid.shape
    return pl.pallas_call(
        functools.partial(attend_back_kernel, n),
        grid=(heads,),
        out_shape=(
            sds(flat, BF), sds(flat, F32), sds(flat, F32), sds(flat, F32), sds(flat, F32),
            sds(flat, BF), sds(flat, BF), sds((chunk, model), BF),
        ),
        in_specs=[pl.BlockSpec(memory_space=pl.ANY), fixed(mid.shape), fixed(ga.shape)]
        + [pl.BlockSpec((ow.shape[0], 128), lambda h: (0, h))]
        + [slab] * 5
        + [square, square, slab, slab, double, square, slab],
        out_specs=[slab] * 7 + [fixed((chunk, model))],
        scratch_shapes=[
            pltpu.VMEM((chunk, model), BF),
            pltpu.VMEM((n - 1, chunk, model), BF),
            pltpu.SemaphoreType.DMA,
            pltpu.SemaphoreType.DMA((n - 1,)),
            pltpu.SemaphoreType.DMA((n - 1,)),
        ],
        compiler_params=pltpu.CompilerParams(
            vmem_limit_bytes=56 * 1024 * 1024, collective_id=4, has_side_effects=True
        ),
        cost_estimate=cost(16),
        name="attend_back",
    )(part, mid, ga, ow, q, k, v, w, beta, t, c, fk, fv, p, x, qt)


def call_keys_back(d, back_v, dq, k, w, beta, t, c, hin, prefix, taps, marks, dk, dv, dw, dwb):
    length, width = k.shape
    whole = pl.BlockSpec(memory_space=pltpu.VMEM)
    return pl.pallas_call(
        keys_back_kernel,
        out_shape=(
            sds((length, 4 * width + 128), BF), sds((HALO, width), F32), sds((HALO, width), BF),
            sds((8, width), F32),
        ),
        in_specs=[whole] * 16,
        out_specs=[whole] * 4,
        compiler_params=params(),
        cost_estimate=cost(10),
        name="keys_back",
    )(d, back_v, dq, k, w, beta, t, c, hin, prefix, taps, marks, dk, dv, dw, dwb)


def exchange(n, name, ident, product, operands, specs, extras, finish, rows_out, wide_type, ride):
    length, model = operands[0].shape[0], operands[1].shape[0]
    chunk = length // n
    given = len(operands)
    many = len(extras)
    share = ride is not None
    riders = ride[:2] if share else ()
    width = ride[2] if share else 0

    def body(*refs):
        operand_refs = refs[:given]
        extra_refs = refs[given : given + many]
        start = given + many + len(riders)
        rider_refs = refs[given + many : start]
        last = start + 1 + len(rows_out)
        out_ref, *row_refs = refs[start:last]
        if share:
            ride_outs = refs[last : last + 3]
            last = last + 3
        send, recv, held, own_part, send_a, recv_a, send_b, recv_b, *small = refs[last:]
        me = lax.axis_index("tensor")
        barrier = pltpu.get_barrier_semaphore()
        peers = [lax.rem(me + i, n) for i in range(1, n)]
        for peer in peers:
            pl.semaphore_signal(
                barrier, inc=1, device_id={"tensor": peer}, device_id_type=pl.DeviceIdType.MESH
            )
        if share:
            core = lax.axis_index("context")
            other = {"context": 1 - core}
            pl.semaphore_signal(
                barrier, inc=1, device_id=other, device_id_type=pl.DeviceIdType.MESH
            )
        pl.semaphore_wait(barrier, n if share else n - 1)

        def rows_of(index):
            return pl.ds(pl.multiple_of(index * chunk, chunk), chunk)

        if share:
            mine_small, slots, result, held_half, send_c, recv_c, send_d, recv_d, core_sems = small
            row_in, half_in = rider_refs
            rows_half = half_in.shape[0]
            own_half_rows = pl.ds(pl.multiple_of(core * rows_half, rows_half), rows_half)
            swap = pltpu.make_async_remote_copy(
                src_ref=half_in, dst_ref=held_half.at[own_half_rows, :],
                send_sem=core_sems.at[0], recv_sem=core_sems.at[1],
                device_id=other, device_id_type=pl.DeviceIdType.MESH,
            )
            swap.start()

        def partial(index):
            return product(rows_of(index), *operand_refs)

        def first_copy(i):
            return pltpu.make_async_remote_copy(
                src_ref=send.at[i], dst_ref=recv.at[i],
                send_sem=send_a.at[i], recv_sem=recv_a.at[i],
                device_id={"tensor": lax.rem(me + i + 1, n)},
                device_id_type=pl.DeviceIdType.MESH,
            )

        def send_step(i, carry):
            value = partial(lax.rem(me + i + 1, n))
            own_part[...] = value

            @pl.when(i < n - 1)
            def go():
                send[i] = value.astype(BF)
                first_copy(i).start()

            return carry

        lax.fori_loop(0, n, send_step, 0)
        total = own_part[...]
        for i in range(n - 1):
            first_copy(i).wait()
            total = total + recv[i].astype(F32)
        mine = rows_of(me)
        done, *row_values = finish(total, mine, *extra_refs)
        held[mine, :] = done.astype(BF)
        second = []
        for i, peer in enumerate(peers):
            copy = pltpu.make_async_remote_copy(
                src_ref=held.at[mine, :], dst_ref=held.at[mine, :],
                send_sem=send_b.at[i], recv_sem=recv_b.at[i],
                device_id={"tensor": peer}, device_id_type=pl.DeviceIdType.MESH,
            )
            copy.start()
            second.append(copy)
        if share:
            fourth = []
            for i, peer in enumerate(peers):
                copy = pltpu.make_async_remote_copy(
                    src_ref=row_in, dst_ref=result.at[mine, :],
                    send_sem=send_d.at[i], recv_sem=recv_d.at[i],
                    device_id={"tensor": peer}, device_id_type=pl.DeviceIdType.MESH,
                )
                copy.start()
                fourth.append(copy)
            mine_small[...] = row_values[-1]
            slots[me] = row_values[-1]
            third = []
            for i, peer in enumerate(peers):
                copy = pltpu.make_async_remote_copy(
                    src_ref=mine_small, dst_ref=slots.at[me],
                    send_sem=send_c.at[i], recv_sem=recv_c.at[i],
                    device_id={"tensor": peer}, device_id_type=pl.DeviceIdType.MESH,
                )
                copy.start()
                third.append(copy)
        for ref, value in zip(row_refs, row_values):
            ref[...] = value
        if share:
            result[mine, :] = row_in[...]
            held_half[own_half_rows, :] = half_in[...]
            swap.wait()
            res_ref, both_ref, down_ref = ride_outs
            both_ref[...] = held_half[...]
            for j in range(down_ref.shape[0] // width):
                turned = held_half[:, 3 * width * j + 2 * width : 3 * width * (j + 1)].T
                down_ref[j * width : (j + 1) * width, :] = turned
            for copy in third:
                copy.wait()
            row_refs[-1][...] = sum(slots[i] for i in range(n))
        for copy in second:
            copy.wait()
        out_ref[...] = held[...].astype(wide_type)
        if share:
            for copy in fourth:
                copy.wait()
            res_ref[...] = result[...]

    ride_shapes = ()
    if share:
        deep_rows, hidden = 2 * ride[1].shape[0], ride[1].shape[1] // 3
        ride_shapes = (
            sds((length, model), BF), sds((deep_rows, 3 * hidden), BF), sds((hidden, deep_rows), BF),
        )
    whole = pl.BlockSpec(memory_space=pltpu.VMEM)
    return pl.pallas_call(
        body,
        out_shape=(sds((length, model), wide_type),)
        + tuple(sds((chunk if r is None else r, model), F32) for r in rows_out)
        + ride_shapes,
        in_specs=[whole if spec is None else spec for spec in specs] + [whole] * (many + len(riders)),
        out_specs=[whole] * (1 + len(rows_out) + len(ride_shapes)),
        scratch_shapes=[
            pltpu.VMEM((n - 1, chunk, model), BF),
            pltpu.VMEM((n - 1, chunk, model), BF),
            pltpu.VMEM((length, model), BF),
            pltpu.VMEM((chunk, model), F32),
            pltpu.SemaphoreType.DMA((n - 1,)),
            pltpu.SemaphoreType.DMA((n - 1,)),
            pltpu.SemaphoreType.DMA((n - 1,)),
            pltpu.SemaphoreType.DMA((n - 1,)),
        ]
        + (
            [
                pltpu.VMEM((8, model), F32),
                pltpu.VMEM((n, 8, model), F32),
                pltpu.VMEM((length, model), BF),
                pltpu.VMEM((2 * ride[1].shape[0], ride[1].shape[1]), BF),
                pltpu.SemaphoreType.DMA((n - 1,)),
                pltpu.SemaphoreType.DMA((n - 1,)),
                pltpu.SemaphoreType.DMA((n - 1,)),
                pltpu.SemaphoreType.DMA((n - 1,)),
                pltpu.SemaphoreType.DMA((2,)),
            ]
            if share
            else []
        ),
        compiler_params=pltpu.CompilerParams(
            vmem_limit_bytes=56 * 1024 * 1024, collective_id=ident, has_side_effects=True
        ),
        cost_estimate=cost(40),
        name=name,
    )(*operands, *extras, *riders)


def inverse_rms(x):
    return lax.rsqrt(jnp.mean(x * x, axis=1, keepdims=True) + 1e-06)


def finish_middle(total, mine, tokens_ref, gain_ref):
    middle = tokens_ref[mine, :].astype(F32) + total
    return middle * inverse_rms(middle) * gain_ref[0:1, :], middle


def norm_back(grad, x, gain):
    r = inverse_rms(x)
    g = grad * gain
    out = r * g - x * (r * r * r * jnp.mean(g * x, axis=1, keepdims=True))
    gain_grad = jnp.sum(grad * x * r, axis=0, keepdims=True)
    return out, jnp.broadcast_to(gain_grad, (8, gain_grad.shape[1]))


def finish_second(total, mine, middle_ref, cot_ref, gain_ref):
    out, gain_grad = norm_back(total, middle_ref[...], gain_ref[0:1, :])
    grad = cot_ref[mine, :].astype(F32) + out
    return grad, grad, gain_grad


def finish_first(total, mine, tokens_ref, grad_ref, gain_ref, second_ref):
    out, gain_grad = norm_back(total, tokens_ref[mine, :].astype(F32), gain_ref[0:1, :])
    row = lax.broadcasted_iota(jnp.int32, gain_grad.shape, 0)
    return grad_ref[...] + out, jnp.where(row == 0, gain_grad, second_ref[...])


def tail_nt(first):
    def product(rows, lhs_ref, rhs_ref):
        width = lhs_ref.shape[1]
        return dot_nt(lhs_ref[rows, :], rhs_ref[:, first : first + width])

    return product


def blocks_nt(width, offset, stride):
    def product(rows, lhs_ref, rhs_ref):
        total = None
        for j in range(lhs_ref.shape[1] // width):
            at = j * stride + offset
            term = dot_nt(lhs_ref[rows, j * width : (j + 1) * width], rhs_ref[:, at : at + width])
            total = term if total is None else total + term
        return total

    return product


def last_kernel(
    deep, cores, x_ref, half_ref, gain_ref, all_ref, out_ref,
    slots, held, send_sem, recv_sem, core_sems,
):
    z, core = lax.axis_index("fsdp"), lax.axis_index("context")
    me = z * cores + core
    count = deep * cores
    barrier = pltpu.get_barrier_semaphore()
    peers = []
    for i in range(1, count):
        peer = lax.rem(me + i, count)
        peers.append({"fsdp": peer // cores, "context": lax.rem(peer, cores)})
    for peer in peers:
        pl.semaphore_signal(barrier, inc=1, device_id=peer, device_id_type=pl.DeviceIdType.MESH)
    pl.semaphore_wait(barrier, count - 1)
    rows_half = half_ref.shape[0]
    own = pl.ds(pl.multiple_of(core * rows_half, rows_half), rows_half)
    swap = pltpu.make_async_remote_copy(
        src_ref=half_ref, dst_ref=held.at[own, :],
        send_sem=core_sems.at[0], recv_sem=core_sems.at[1],
        device_id={"context": 1 - core}, device_id_type=pl.DeviceIdType.MESH,
    )
    swap.start()
    copies = []
    for i, peer in enumerate(peers):
        copy = pltpu.make_async_remote_copy(
            src_ref=x_ref.at[peer["fsdp"]], dst_ref=slots.at[me],
            send_sem=send_sem.at[i], recv_sem=recv_sem.at[i],
            device_id=peer, device_id_type=pl.DeviceIdType.MESH,
        )
        copy.start()
        copies.append(copy)
    slots[me] = x_ref[z]
    held[own, :] = half_ref[...]
    swap.wait()
    out_ref[...] = held[:, : out_ref.shape[0]].T
    all_ref[...] = held[...]
    for copy in copies:
        copy.wait()
    gain_ref[...] = sum(slots[i] for i in range(count))


def call_last(x, half, inner, cores):
    deep, eight, rows = x.shape
    count = deep * cores
    full = cores * half.shape[0]
    whole = pl.BlockSpec(memory_space=pltpu.VMEM)
    return pl.pallas_call(
        functools.partial(last_kernel, deep, cores),
        out_shape=(
            sds((eight, rows), F32), sds((full, half.shape[1]), BF), sds((inner, full), BF),
        ),
        in_specs=[whole] * 2,
        out_specs=[whole] * 3,
        scratch_shapes=[
            pltpu.VMEM((count, eight, rows), F32),
            pltpu.VMEM((full, half.shape[1]), BF),
            pltpu.SemaphoreType.DMA((count - 1,)),
            pltpu.SemaphoreType.DMA((count - 1,)),
            pltpu.SemaphoreType.DMA((2,)),
        ],
        compiler_params=pltpu.CompilerParams(collective_id=5, has_side_effects=True),
        cost_estimate=cost(8),
        name="last",
    )(x, half)


def write_kernel(
    width, res_in, grad_in, both_in, down_in, all_in, turn_in,
    res_ref, grad_ref, gate_ref, up_ref, down_ref, out_ref, q_ref, k_ref, v_ref, h_ref, side_ref,
):
    res_ref[...] = res_in[...]
    grad_ref[...] = grad_in[...].astype(F32)
    for j in range(gate_ref.shape[1] // width):
        at, to = 3 * width * j, slice(j * width, (j + 1) * width)
        gate_ref[:, to] = both_in[:, at : at + width].astype(F32)
        up_ref[:, to] = both_in[:, at + width : at + 2 * width].astype(F32)
    down_ref[...] = down_in[...].astype(F32)
    out_ref[...] = turn_in[...].astype(F32)
    inner = q_ref.shape[1]
    for i, ref in enumerate((q_ref, k_ref, v_ref, h_ref)):
        ref[...] = all_in[:, (i + 1) * inner : (i + 2) * inner].astype(F32)
    side_ref[...] = all_in[:, 5 * inner :].astype(F32)


def call_write(width, res, grad, both, down, packed, turned):
    rows = both.shape[0]
    hidden, inner = down.shape[0], turned.shape[0]
    steps = next(count for count in (4, 2, 1) if rows // count % 16 == 0)

    def spec(shape):
        return pl.BlockSpec((shape[0] // steps, shape[1]), lambda i: (i, 0))

    outs = (
        sds(res.shape, BF), sds(grad.shape, F32), sds((rows, hidden), F32),
        sds((rows, hidden), F32), sds(down.shape, F32), sds(turned.shape, F32),
    )
    outs = outs + (sds((rows, inner), F32),) * 4
    outs = outs + (sds((rows, packed.shape[1] - 5 * inner), F32),)
    args = (res, grad, both, down, packed, turned)
    return pl.pallas_call(
        functools.partial(write_kernel, width),
        grid=(steps,),
        out_shape=outs,
        in_specs=[spec(x.shape) for x in args],
        out_specs=[spec(x.shape) for x in outs],
        compiler_params=params(),
        cost_estimate=cost(6),
        name="write",
    )(*args)


def ffn_kernel(n_ref, cot_ref, w_ref, part_ref, gb_ref, gw_ref, nt, ct, acc):
    width = w_ref.shape[1] // 3

    @pl.when(pl.program_id(0) == 0)
    def turn():
        nt[...] = n_ref[...].T
        ct[...] = cot_ref[...].T
        acc[...] = jnp.zeros_like(acc)

    both = dot_nn(n_ref[...], w_ref[:, : 2 * width])
    gate, up = both[:, :width], both[:, width:]
    back = dot_nn(cot_ref[...], w_ref[:, 2 * width :])
    sig = jax.nn.sigmoid(gate)
    act = gate * sig
    hidden = (act * up).astype(BF)
    acc[...] += dot_nt(hidden, w_ref[:, 2 * width :])
    grad = jnp.concatenate(
        [(back * up * (sig + act * (1.0 - sig))).astype(BF), (back * act).astype(BF)], axis=1
    )
    gb_ref[...] = grad
    gw_ref[:, : 2 * width] = dot_nn(nt[...], grad).astype(BF)
    gw_ref[:, 2 * width :] = dot_nn(ct[...], hidden).astype(BF)

    @pl.when(pl.program_id(0) == pl.num_programs(0) - 1)
    def close():
        part_ref[...] = acc[...].astype(BF)


def call_ffn(normed, cot, weights, width):
    length, model = normed.shape
    steps = weights.shape[1] // (3 * width)
    return pl.pallas_call(
        ffn_kernel,
        grid=(steps,),
        out_shape=(
            sds((length, model), BF),
            sds((length, steps * 2 * width), BF),
            sds(weights.shape, BF),
        ),
        in_specs=[
            fixed(normed.shape), fixed(cot.shape),
            pl.BlockSpec((model, 3 * width), lambda j: (0, j)),
        ],
        out_specs=[
            fixed((length, model)),
            pl.BlockSpec((length, 2 * width), lambda j: (0, j)),
            pl.BlockSpec((model, 3 * width), lambda j: (0, j)),
        ],
        scratch_shapes=[
            pltpu.VMEM((model, length), BF),
            pltpu.VMEM((model, length), BF),
            pltpu.VMEM((length, model), F32),
        ],
        compiler_params=params(),
        cost_estimate=cost(14),
        name="ffn",
    )(normed, cot, weights)


def grads_kernel(lane, n_ref, ga_ref, d_ref, m_ref, conv_ref, out_ref):
    inner = m_ref.shape[1]
    main = d_ref.shape[1] - 128
    out_ref[:, :inner] = dot_tn(ga_ref[...], m_ref[...]).astype(BF)
    out_ref[:, inner : inner + main] = dot_tn(n_ref[...], d_ref[:, :main]).astype(BF)
    side = dot_tn(n_ref[...], d_ref[:, main:])
    lanes = lax.broadcasted_iota(jnp.int32, side.shape, 1)
    out_ref[:, inner + main :] = jnp.where(lanes == lane, conv_ref[...], side).astype(BF)


def call_grads(lane, normed, ga, dproj, mixed, dconv):
    length, model = normed.shape
    block = 384
    wide = dproj.shape[1] + mixed.shape[1]
    part = pl.BlockSpec((length, block), lambda i: (0, i))
    return pl.pallas_call(
        functools.partial(grads_kernel, lane),
        grid=(model // block,),
        out_shape=sds((model, wide), BF),
        in_specs=[
            part, part, fixed(dproj.shape), fixed(mixed.shape),
            pl.BlockSpec((block, 1), lambda i: (i, 0)),
        ],
        out_specs=pl.BlockSpec((block, wide), lambda i: (i, 0)),
        compiler_params=params(),
        cost_estimate=cost(7),
        name="grads",
    )(normed, ga, dproj, mixed, dconv)


def shift_to(value, axis, steps):
    count = lax.axis_size(axis)
    leading, last = (max(0, -steps), min(count, count - steps))
    return lax.ppermute(value, axis, [(at, at + steps) for at in range(leading, last)])


def own_half(value):
    rows = value.shape[0] // lax.axis_size("context")
    return lax.dynamic_slice_in_dim(value, lax.axis_index("context") * rows, rows, axis=0)


def gather_rows(value):
    return lax.all_gather(own_half(value), ("fsdp", "context"), axis=0, tiled=True)


def scatter_half(value):
    return lax.psum_scatter(value, ("fsdp", "context"), scatter_dimension=0, tiled=True)


FBLOCK = 256


def on_device(
    tokens,
    segments,
    cotangent,
    query_weight,
    key_weight,
    value_weight,
    house_weight,
    beta_weight,
    conv_weight,
    output_weight,
    gate_weight,
    up_weight,
    down_weight,
    first_gain,
    second_gain,
):
    seq_count, length, model = tokens.shape
    rows = first_gain.shape[0]
    deep = lax.axis_size("fsdp")
    inner = query_weight.shape[1]
    heads, tap_count, chans = conv_weight.shape
    assert seq_count == 1 and heads * tap_count * chans == rows
    side = jnp.concatenate(
        [
            beta_weight,
            first_gain[:, None],
            second_gain[:, None],
            conv_weight.reshape(rows, 1),
            jnp.zeros((rows, 128 - heads - 3), BF),
        ],
        axis=1,
    )
    pack = gather_rows(
        jnp.concatenate(
            [output_weight.T, query_weight, key_weight, value_weight, house_weight, side], axis=1
        )
    )
    hidden_width = gate_weight.shape[1]
    steps = hidden_width // FBLOCK
    down_t = down_weight.T
    ffn_w = gather_rows(
        jnp.concatenate(
            [
                part[:, j * FBLOCK : (j + 1) * FBLOCK]
                for j in range(steps)
                for part in (gate_weight, up_weight, down_t)
            ],
            axis=1,
        )
    )
    side_full = pack[:, 5 * inner :]
    gain_one = side_full[:, heads].astype(F32)
    gain_two = side_full[:, heads + 1].astype(F32)
    taps = jnp.transpose(
        side_full[:, heads + 2].reshape(deep, heads, tap_count, chans), (2, 1, 0, 3)
    ).reshape(tap_count, inner).astype(F32)

    tags = (segments[0] + 1).astype(F32)
    far_tags = shift_to(tags, "context", 1)
    near_tags = jnp.concatenate([far_tags[length - tap_count + 1 :], tags])
    marks = jnp.stack(
        [
            near_tags[tap_count - 1 - lag : tap_count - 1 - lag + length] == tags
            for lag in range(tap_count)
        ],
        axis=1,
    ).astype(F32)

    stream = tokens[0].astype(F32)
    scale_one = lax.rsqrt(jnp.mean(stream * stream, axis=1, keepdims=True) + 1e-06)
    normed = (stream * scale_one * gain_one).astype(BF)
    proj = dot_nn(normed, pack[:, inner : 5 * inner]).astype(BF)
    beta_raw = dot_nn(normed, side_full)[:, :heads]
    beta = jnp.repeat(2.0 * jax.nn.sigmoid(beta_raw), 128, axis=1)
    q, k, v, hin = (proj[:, i * inner : (i + 1) * inner] for i in range(4))
    prefix = shift_to(hin[length - HALO :], "context", 1)
    w, t, c, sent = call_prep(k, hin, prefix, taps, marks, beta)
    far_k = shift_to(sent, "context", 1)
    far_v = shift_to(v, "context", 1)
    mixed, probs, x, qt = call_attend(
        q, k, v, w, beta, t, c, far_k, far_v, tags[:, None], jnp.stack([tags, far_tags])
    )
    n = lax.axis_size("tensor")
    rows_one = jnp.broadcast_to(gain_one[None, :], (8, model))
    rows_two = jnp.broadcast_to(gain_two[None, :], (8, model))
    normed_two, middle = exchange(
        n, "sum_mixed", 1, tail_nt(0), (mixed, pack),
        (None, None), (tokens[0], rows_two),
        finish_middle, (None,), BF, None,
    )
    cot = cotangent[0]
    part, grad_both, grad_ffn = call_ffn(normed_two, cot, ffn_w, FBLOCK)
    grad_both, grad_ffn = lax.optimization_barrier((grad_both, grad_ffn))
    grad_ffn = scatter_half(grad_ffn)
    grad_attn, grad_middle, grad_second = exchange(
        n, "sum_second", 2, blocks_nt(2 * FBLOCK, 0, 3 * FBLOCK), (grad_both, ffn_w),
        (None, None), (middle, cot, rows_two), finish_second, (None, 8), BF, None,
    )

    dq, dk, dv, dw, dwb, dfk, dfv, finished = call_attend_back(
        n, part, middle, grad_attn, pack, q, k, v, w, beta, t, c, far_k, far_v, probs, x, qt
    )
    back_k = shift_to(dfk, "context", -1)
    back_v = shift_to(dfv, "context", -1)
    dproj, tail, dpre, dtap = call_keys_back(
        back_k, back_v, dq, k, w, beta, t, c, hin, prefix, taps, marks, dk, dv, dw, dwb
    )
    back_pre = shift_to(dpre, "context", -1).astype(F32)
    dproj = lax.dynamic_update_slice(
        dproj, (tail + back_pre).astype(BF), (length - HALO, 3 * inner)
    )
    dconv = jnp.transpose(
        dtap[:tap_count].reshape(tap_count, heads, deep, chans), (2, 1, 0, 3)
    ).reshape(model, 1)
    grad_pack = call_grads(heads + 2, normed, grad_attn, dproj, mixed, dconv)
    dproj, grad_pack, grad_ffn = lax.optimization_barrier((dproj, grad_pack, grad_ffn))
    grad_pack = scatter_half(grad_pack)
    grad_input, gains, result, both, down = exchange(
        n, "sum_first", 3, tail_nt(inner), (dproj, pack), (None, None),
        (tokens[0], grad_middle, rows_one, grad_second), finish_first, (8,), BF,
        (finished, grad_ffn, FBLOCK),
    )
    gains = jnp.transpose(gains.reshape(8, deep, rows), (1, 0, 2))
    gains, packed, turned = call_last(gains, grad_pack, inner, lax.axis_size("context"))
    (
        result, grad_input, gate_grad, up_grad, down_grad, out_grad,
        q_grad, k_grad, v_grad, h_grad, side_grad,
    ) = call_write(FBLOCK, result, grad_input, both, down, packed, turned)
    return (
        result.reshape(tokens.shape),
        grad_input.reshape(tokens.shape),
        q_grad,
        k_grad,
        v_grad,
        h_grad,
        side_grad[:, :heads],
        side_grad[:, heads + 2].reshape(conv_weight.shape),
        out_grad,
        gate_grad,
        up_grad,
        down_grad,
        gains[0],
        gains[1],
    )


def solution(mesh):
    in_specs = (
        P("fsdp", "context", None),
        P("fsdp", "context"),
        P("fsdp", "context", None),
        P("fsdp", "tensor"),
        P("fsdp", "tensor"),
        P("fsdp", "tensor"),
        P("fsdp", "tensor"),
        P("fsdp", "tensor"),
        P("tensor", None, "fsdp"),
        P("tensor", "fsdp"),
        P("fsdp", "tensor"),
        P("fsdp", "tensor"),
        P("tensor", "fsdp"),
        P("fsdp"),
        P("fsdp"),
    )
    out_specs = (
        P("fsdp", "context", None),
        P("fsdp", "context", None),
        P("fsdp", "tensor"),
        P("fsdp", "tensor"),
        P("fsdp", "tensor"),
        P("fsdp", "tensor"),
        P("fsdp", "tensor"),
        P("tensor", None, "fsdp"),
        P("tensor", "fsdp"),
        P("fsdp", "tensor"),
        P("fsdp", "tensor"),
        P("tensor", "fsdp"),
        P("fsdp"),
        P("fsdp"),
    )
    return jax.shard_map(
        on_device, mesh=mesh, in_specs=in_specs, out_specs=out_specs, check_vma=False
    )
```
